256 devices in a mesh: row: 32 (over z, y_lo, core), pair: 8 (over x, y_hi).
Axes of the slice: x: 4, y: 4 (y_hi: 2, y_lo: 2; y = y_hi * 2 + y_lo), z: 8, core: 2. Of those that a mesh axis runs over, the one named last changes fastest.
Arguments:
- panel: float32 [16384, 2048], P('row', 'pair'), may hold values from -200 to 200, as said below
Outputs:
- rotated: float32 [16384, 2048], P('row', 'pair')
The draws below stay inside these ranges and needn't reach their ends.
Inputs may be any that keep to these rules, and one draw needn't show every extreme that they name: `panel`: real entries.
All inputs are finite; a program needn't handle non-finite values.
Results may differ from the reference program's by a relative error of at most 0.00016.
Values sent between devices are 32-bit elements; how exact they have to be, the bound alone decides.
No kernel may reach another device: no remote copies, remote signals or barrier semaphores. Data moves between devices by JAX's collectives and lax.ppermute only.
A program may use at most 64 MiB of HBM per device.

```python
import jax
import jax.numpy as jnp
from jax import lax

BLK = 128
STEPS = 3
ROWS = 16384
COLS = 2048


def draw_panel(key, part):
    k_noise, k_factor, k_mix, k_rough = jax.random.split(jax.random.fold_in(key, 11), 4)
    noise = jax.random.normal(k_noise, (ROWS, COLS), jnp.float32)
    mix = 0.5 * jax.random.normal(k_mix, (4, COLS), jnp.float32)
    factor = jax.random.normal(k_factor, (ROWS, 4), jnp.float32)
    rough = jnp.exp(jax.random.uniform(k_rough, (ROWS,), jnp.float32, -0.3, 0.3))
    place = jnp.arange(ROWS, dtype=jnp.float32) / ROWS
    scale = jnp.sqrt(1.0 + 2.0 * place) * rough
    return scale[:, None] * (noise + jnp.dot(factor, mix))


def setup_inputs(seed: int = 0) -> dict:
    key_list = jax.random.split(jax.random.key(seed), 2)
    panel = draw_panel(jax.random.fold_in(key_list[1], 71), 0)
    return {"panel": panel}


HIGH = lax.Precision.HIGHEST

def rotation(gram, blk):
    diag_all = jnp.diagonal(gram)
    scale = lax.rsqrt(diag_all + 1e-06)
    cosine = gram[:blk, blk:] * scale[:blk, None] * scale[None, blk:]
    damped = 0.25 * cosine
    zero = jnp.zeros((blk, blk), jnp.float32)
    skew = jnp.concatenate([jnp.concatenate([zero, damped], 1), jnp.concatenate([-damped.T, zero], 1)], 0)
    eye = jnp.eye(2 * blk, dtype=jnp.float32)
    normal = eye + jnp.dot(skew.T, skew, precision=HIGH)
    plus = eye + skew
    factor = jnp.linalg.cholesky(normal)
    return jax.scipy.linalg.cho_solve((factor, True), jnp.dot(plus, plus, precision=HIGH))

def reference(panel):
    pairs = COLS // (2 * BLK)
    current = panel.reshape(ROWS, pairs, 2 * BLK)
    for step in range(STEPS):
        gram = jnp.einsum('rpi,rpj->pij', current, current, precision=HIGH)
        cayley = jax.vmap(lambda g: rotation(g, BLK))(gram)
        current = jnp.einsum('rpi,pij->rpj', current, cayley, precision=HIGH)
        first = current[:, :, :BLK]
        second = jnp.roll(current[:, :, BLK:], 1, axis=1)
        current = jnp.concatenate([first, second], 2)
    return current.reshape(ROWS, COLS)
```

```python
import jax
import jax.numpy as jnp
from jax import lax
from jax.experimental import pallas as pl
from jax.experimental.pallas import tpu as pltpu
from jax.sharding import PartitionSpec as P

STEPS = 3

BF16 = jnp.bfloat16
F32 = jnp.float32
HIGH = lax.Precision.HIGHEST

QUAD = 4
PAD = 8


def split(x):
    hi = x.astype(BF16)
    return hi, (x - hi.astype(F32)).astype(BF16)


def left3(x):
    return jnp.concatenate(split(x), 1)


def right3(x):
    hi, lo = split(x)
    top = jnp.concatenate([hi, lo], 1)
    low = jnp.concatenate([hi, jnp.zeros_like(hi)], 1)
    return jnp.concatenate([top, low], 0)


def times3(left, right):
    out = jnp.dot(left, right, preferred_element_type=F32)
    n = out.shape[1] // 2
    return out[:, :n] + out[:, n:]


def times(a, b):
    return jnp.dot(a, b, precision=HIGH, preferred_element_type=F32)


def rotation(cross, diag_a, diag_b):
    n = cross.shape[0]
    scale_a = lax.rsqrt(diag_a + 1e-06)
    scale_b = lax.rsqrt(diag_b + 1e-06)
    d = 0.25 * (cross * jnp.transpose(jnp.broadcast_to(scale_a, (n, n))) * scale_b)
    dt = jnp.transpose(d)
    shape = (n, n)
    eye = jnp.where(
        lax.broadcasted_iota(jnp.int32, shape, 0) == lax.broadcasted_iota(jnp.int32, shape, 1),
        1.0,
        0.0,
    ).astype(F32)
    base = eye + times(d, dt)
    top = 1.0 + 1.001 * (0.25 * n) ** 2
    start = 2.0 / (1.0 + top)
    gap = (top - 1.0) / (top + 1.0)
    y = start * base
    x = None
    while gap > 1e-3:
        z = 2.0 * eye - y
        stretch = 2.0 / (2.0 - gap * gap)
        right = right3(z)
        if x is None:
            y = stretch * times3(left3(y), right)
            x = (stretch * start) * z
        else:
            both = stretch * times3(jnp.concatenate([left3(x), left3(y)], 0), right)
            x, y = both[:n], both[n:]
        gap = gap * gap / (2.0 - gap * gap)
    for _ in range(2):
        x = times(x, 2.0 * eye - times(base, x))
    md = times(x, d)
    mixed = 2.0 * md
    return 2.0 * x - eye, mixed, -jnp.transpose(mixed), eye - 2.0 * times(dt, md)


def gram_kernel(core_ref, a_ref, b_ref, mine_ref, other_ref, cross_ref):
    a = a_ref[...]
    b = b_ref[...]
    n = a.shape[1]
    half = n // 2
    a_hi, a_lo = split(jnp.transpose(a))
    b_hi, b_lo = split(b)
    wide = jnp.dot(a_hi, jnp.concatenate([b_hi, b_lo], 1), preferred_element_type=F32)
    cross = wide[:, :n] + wide[:, n:] + jnp.dot(a_lo, b_hi, preferred_element_type=F32)
    cross_ref[:half] = cross[:half]
    cross_ref[half + PAD : n + PAD] = cross[half:]
    cross_ref[half : half + PAD] = jnp.broadcast_to(jnp.sum(a * a, 0, keepdims=True), (PAD, n))
    cross_ref[n + PAD :] = jnp.broadcast_to(jnp.sum(b * b, 0, keepdims=True), (PAD, n))
    core = core_ref[0]
    step = half + PAD
    mine_ref[...] = cross_ref[pl.ds(pl.multiple_of(core * step, 8), step), :]
    other_ref[...] = cross_ref[pl.ds(pl.multiple_of((1 - core) * step, 8), step), :]


def turn_kernel(core_ref, mine_ref, other_ref, a_ref, b_ref, a_out, b_out):
    n = a_ref.shape[1]
    half = n // 2
    first = core_ref[0] == 0
    mine = mine_ref[...]
    other = other_ref[...]
    low = jnp.where(first, mine, other)
    high = jnp.where(first, other, mine)
    cross = jnp.concatenate([low[:half], high[:half]], 0)
    c11, c12, c21, c22 = rotation(cross, low[half : half + 1], high[half : half + 1])
    cayley = jnp.concatenate(
        [jnp.concatenate([c11, c12], 1), jnp.concatenate([c21, c22], 1)], 0
    )
    x_hi, x_lo = split(jnp.concatenate([a_ref[...], b_ref[...]], 1))
    c_hi, c_lo = split(cayley)
    out = (
        jnp.dot(x_hi, c_hi, preferred_element_type=F32)
        + jnp.dot(x_lo, c_hi, preferred_element_type=F32)
        + jnp.dot(x_hi, c_lo, preferred_element_type=F32)
    )
    a_out[...] = out[:, :n]
    b_out[...] = out[:, n:]


def spec_list(count):
    return [pl.BlockSpec(memory_space=pltpu.SMEM)] + [
        pl.BlockSpec(memory_space=pltpu.VMEM)
    ] * count


def gram(core, a, b):
    n = a.shape[1]
    half = jax.ShapeDtypeStruct((n // 2 + PAD, n), F32)
    return pl.pallas_call(
        gram_kernel,
        out_shape=[half, half],
        in_specs=spec_list(2),
        scratch_shapes=[pltpu.VMEM((n + 2 * PAD, n), F32)],
        name="gram",
    )(core, a, b)


def turn(core, mine, other, a, b):
    return pl.pallas_call(
        turn_kernel,
        out_shape=[jax.ShapeDtypeStruct(a.shape, F32)] * 2,
        in_specs=spec_list(4),
        name="turn",
    )(core, mine, other, a, b)


def swapped(x, flip):
    peers = range(lax.axis_size("row"))
    return lax.ppermute(x, "row", [(i, i ^ flip) for i in peers])


def summed_halves(mine, other):
    rows = lax.axis_size("row")
    line = rows // QUAD
    quad_sum = (mine + swapped(mine, 2)) + (swapped(other, 1) + swapped(other, 3))
    groups = [[j + QUAD * i for i in range(line)] for j in range(QUAD)]
    parts = lax.all_to_all(
        jnp.broadcast_to(quad_sum[None], (line, *quad_sum.shape)),
        "row",
        0,
        0,
        tiled=True,
        axis_index_groups=groups,
    )
    whole = jnp.sum(parts, 0)
    return whole, swapped(whole, 1)


def shifted(block):
    devices = range(lax.axis_size("pair"))
    route = [((i - 1) % len(devices), i) for i in devices]
    return lax.ppermute(block, "pair", route)


def local(panel):
    blk = panel.shape[1] // 2
    core = (lax.axis_index("row") % 2).astype(jnp.int32).reshape(1)
    a, b = panel[:, :blk], panel[:, blk:]
    for step in range(STEPS):
        mine, other = gram(core, a, b)
        mine, other = summed_halves(mine, other)
        a, b = turn(core, mine, other, a, b)
        b = shifted(b)
    return jnp.concatenate([a, b], 1)


def solution(mesh):
    return jax.shard_map(
        local,
        mesh=mesh,
        in_specs=(P("row", "pair"),),
        out_specs=P("row", "pair"),
        check_vma=False,
    )
```

```python
import jax
import jax.numpy as jnp
from jax import lax
from jax.experimental import pallas as pl
from jax.experimental.pallas import tpu as pltpu
from jax.sharding import PartitionSpec as P

STEPS = 3

BF16 = jnp.bfloat16
F32 = jnp.float32
HIGH = lax.Precision.HIGHEST

QUAD = 4
PAD = 8


def split(x):
    hi = x.astype(BF16)
    return hi, (x - hi.astype(F32)).astype(BF16)


def left3(x):
    return jnp.concatenate(split(x), 1)


def right3(x):
    hi, lo = split(x)
    top = jnp.concatenate([hi, lo], 1)
    low = jnp.concatenate([hi, jnp.zeros_like(hi)], 1)
    return jnp.concatenate([top, low], 0)


def times3(left, right):
    out = jnp.dot(left, right, preferred_element_type=F32)
    n = out.shape[1] // 2
    return out[:, :n] + out[:, n:]


def times(a, b):
    return jnp.dot(a, b, precision=HIGH, preferred_element_type=F32)


def rotation(cross, diag_a, diag_b):
    n = cross.shape[0]
    scale_a = lax.rsqrt(diag_a + 1e-06)
    scale_b = lax.rsqrt(diag_b + 1e-06)
    d = 0.25 * (cross * jnp.transpose(jnp.broadcast_to(scale_a, (n, n))) * scale_b)
    dt = jnp.transpose(d)
    shape = (n, n)
    eye = jnp.where(
        lax.broadcasted_iota(jnp.int32, shape, 0) == lax.broadcasted_iota(jnp.int32, shape, 1),
        1.0,
        0.0,
    ).astype(F32)
    base = eye + times(d, dt)
    top = 1.0 + 1.001 * (0.25 * n) ** 2
    start = 2.0 / (1.0 + top)
    gap = (top - 1.0) / (top + 1.0)
    y = start * base
    x = None
    while gap > 1e-3:
        z = 2.0 * eye - y
        stretch = 2.0 / (2.0 - gap * gap)
        right = right3(z)
        if x is None:
            y = stretch * times3(left3(y), right)
            x = (stretch * start) * z
        else:
            both = stretch * times3(jnp.concatenate([left3(x), left3(y)], 0), right)
            x, y = both[:n], both[n:]
        gap = gap * gap / (2.0 - gap * gap)
    for _ in range(2):
        x = times(x, 2.0 * eye - times(base, x))
    md = times(x, d)
    mixed = 2.0 * md
    return 2.0 * x - eye, mixed, -jnp.transpose(mixed), eye - 2.0 * times(dt, md)


def message(diag_a, diag_b, cross, core, cross_ref, mine_ref, other_ref):
    n = cross.shape[0]
    half = n // 2
    step = half + PAD
    cross_ref[:half] = cross[:half]
    cross_ref[step : step + half] = cross[half:]
    cross_ref[half:step] = jnp.broadcast_to(diag_a, (PAD, n))
    cross_ref[step + half :] = jnp.broadcast_to(diag_b, (PAD, n))
    mine_ref[...] = cross_ref[pl.ds(pl.multiple_of(core * step, 8), step), :]
    other_ref[...] = cross_ref[pl.ds(pl.multiple_of((1 - core) * step, 8), step), :]


def both_blocks(refs):
    if len(refs) == 1:
        n = refs[0].shape[1] // 2
        return refs[0][:, :n], refs[0][:, n:]
    return refs[0][...], refs[1][...]


def gram_kernel(core_ref, *refs):
    *blocks, mine_ref, other_ref, cross_ref = refs
    a, b = both_blocks(blocks)
    n = a.shape[1]
    a_hi, a_lo = split(jnp.transpose(a))
    b_hi, b_lo = split(b)
    wide = jnp.dot(a_hi, jnp.concatenate([b_hi, b_lo], 1), preferred_element_type=F32)
    cross = wide[:, :n] + wide[:, n:] + jnp.dot(a_lo, b_hi, preferred_element_type=F32)
    message(
        jnp.sum(a * a, 0, keepdims=True),
        jnp.sum(b * b, 0, keepdims=True),
        cross,
        core_ref[0],
        cross_ref,
        mine_ref,
        other_ref,
    )


def turn_kernel(core_ref, mine_ref, other_ref, *refs):
    *blocks, a_out, b_out = refs
    a, b = both_blocks(blocks)
    n = a.shape[1]
    half = n // 2
    first = core_ref[0] == 0
    mine = mine_ref[...]
    other = other_ref[...]
    low = jnp.where(first, mine, other)
    high = jnp.where(first, other, mine)
    cross = jnp.concatenate([low[:half], high[:half]], 0)
    c11, c12, c21, c22 = rotation(cross, low[half : half + 1], high[half : half + 1])
    x_hi, x_lo = split(jnp.concatenate([a, b], 1))
    for out_ref, top, low in ((b_out, c12, c22), (a_out, c11, c21)):
        c_hi, c_lo = split(jnp.concatenate([top, low], 0))
        wide = jnp.dot(x_hi, jnp.concatenate([c_hi, c_lo], 1), preferred_element_type=F32)
        out_ref[...] = (
            wide[:, :n] + wide[:, n:] + jnp.dot(x_lo, c_hi, preferred_element_type=F32)
        )


def in_specs(count):
    return [pl.BlockSpec(memory_space=pltpu.SMEM)] + [
        pl.BlockSpec(memory_space=pltpu.VMEM)
    ] * count


def near(x):
    return pltpu.with_memory_space_constraint(x, pltpu.VMEM)


def gram(core, blocks, n):
    half = pltpu.VMEM((n // 2 + PAD, n), F32)
    return pl.pallas_call(
        gram_kernel,
        out_shape=[half, half],
        in_specs=in_specs(len(blocks)),
        scratch_shapes=[pltpu.VMEM((n + 2 * PAD, n), F32)],
        name="gram",
    )(core, *map(near, blocks))


def turn(core, mine, other, blocks, n):
    return pl.pallas_call(
        turn_kernel,
        out_shape=[pltpu.VMEM((blocks[0].shape[0], n), F32)] * 2,
        in_specs=in_specs(2 + len(blocks)),
        name="turn",
    )(core, near(mine), near(other), *map(near, blocks))


def from_row(x, source):
    devices = range(lax.axis_size("row"))
    line = len(devices) // QUAD
    route = []
    for i in devices:
        z, y_lo, core = source(i // QUAD, i // 2 % 2, i % 2)
        route.append((z % line * QUAD + y_lo * 2 + core, i))
    return lax.ppermute(x, "row", route)


def side(z):
    return 1 if z % 2 else -1


def summed_halves(mine, other):
    x = mine + from_row(other, lambda z, y, c: (z, y, 1 - c))
    x = (
        (x + from_row(x, lambda z, y, c: (z ^ 1, y, c)))
        + from_row(x, lambda z, y, c: (z, 1 - y, c))
        + from_row(x, lambda z, y, c: (z ^ 1, 1 - y, c))
    )
    x = (
        (x + from_row(x, lambda z, y, c: (z + side(z), y, c)))
        + from_row(x, lambda z, y, c: (z - 2 * side(z), y, c))
        + from_row(x, lambda z, y, c: (z + 3 * side(z), y, c))
    )
    return x, from_row(x, lambda z, y, c: (z, y, 1 - c))


def shifted(block):
    devices = range(lax.axis_size("pair"))
    route = [((i - 1) % len(devices), i) for i in devices]
    return lax.ppermute(block, "pair", route)


def local(panel):
    n = panel.shape[1] // 2
    core = (lax.axis_index("row") & 1).astype(jnp.int32).reshape(1)
    blocks = [panel]
    for step in range(STEPS):
        mine, other = gram(core, blocks, n)
        mine, other = summed_halves(mine, other)
        a, b = turn(core, mine, other, blocks, n)
        blocks = [a, shifted(b)]
    return jnp.concatenate(blocks, 1)


def solution(mesh):
    return jax.shard_map(
        local,
        mesh=mesh,
        in_specs=(P("row", "pair"),),
        out_specs=P("row", "pair"),
        check_vma=False,
    )
```

```python
import jax
import jax.numpy as jnp
from jax import lax
from jax.experimental import pallas as pl
from jax.experimental.pallas import tpu as pltpu
from jax.sharding import PartitionSpec as P


STEPS = 3

BF16 = jnp.bfloat16
F32 = jnp.float32
HIGH = lax.Precision.HIGHEST

QUAD = 4
PAD = 8


def split(x):
    hi = x.astype(BF16)
    return hi, (x - hi.astype(F32)).astype(BF16)


def left3(x):
    return jnp.concatenate(split(x), 1)


def right3(x):
    hi, lo = split(x)
    top = jnp.concatenate([hi, lo], 1)
    low = jnp.concatenate([hi, jnp.zeros_like(hi)], 1)
    return jnp.concatenate([top, low], 0)


def times3(left, right):
    out = jnp.dot(left, right, preferred_element_type=F32)
    n = out.shape[1] // 2
    return out[:, :n] + out[:, n:]


def times(a, b):
    return jnp.dot(a, b, precision=HIGH, preferred_element_type=F32)


def rotation(cross, diag_a, diag_b):
    n = cross.shape[0]
    scale_a = lax.rsqrt(diag_a + 1e-06)
    scale_b = lax.rsqrt(diag_b + 1e-06)
    d = 0.25 * (cross * jnp.transpose(jnp.broadcast_to(scale_a, (n, n))) * scale_b)
    dt = jnp.transpose(d)
    shape = (n, n)
    eye = jnp.where(
        lax.broadcasted_iota(jnp.int32, shape, 0) == lax.broadcasted_iota(jnp.int32, shape, 1),
        1.0,
        0.0,
    ).astype(F32)
    base = eye + times(d, dt)
    top = 1.0 + 1.001 * (0.25 * n) ** 2
    start = 2.0 / (1.0 + top)
    gap = (top - 1.0) / (top + 1.0)
    y = start * base
    x = None
    while gap > 1e-3:
        z = 2.0 * eye - y
        stretch = 2.0 / (2.0 - gap * gap)
        right = right3(z)
        if x is None:
            y = stretch * times3(left3(y), right)
            x = (stretch * start) * z
        else:
            both = stretch * times3(jnp.concatenate([left3(x), left3(y)], 0), right)
            x, y = both[:n], both[n:]
        gap = gap * gap / (2.0 - gap * gap)
    for _ in range(2):
        x = times(x, 2.0 * eye - times(base, x))
    md = times(x, d)
    mixed = 2.0 * md
    return 2.0 * x - eye, mixed, -jnp.transpose(mixed), eye - 2.0 * times(dt, md)


def message(diag_a, diag_b, cross, core, cross_ref, mine_ref, other_ref):
    n = cross.shape[0]
    half = n // 2
    step = half + PAD
    cross_ref[:half] = cross[:half]
    cross_ref[step : step + half] = cross[half:]
    cross_ref[half:step] = jnp.broadcast_to(diag_a, (PAD, n))
    cross_ref[step + half :] = jnp.broadcast_to(diag_b, (PAD, n))
    mine_ref[...] = cross_ref[pl.ds(pl.multiple_of(core * step, 8), step), :]
    other_ref[...] = cross_ref[pl.ds(pl.multiple_of((1 - core) * step, 8), step), :]


def both_blocks(refs):
    if len(refs) == 1:
        n = refs[0].shape[1] // 2
        return refs[0][:, :n], refs[0][:, n:]
    return refs[0][...], refs[1][...]


def gram_kernel(core_ref, *refs):
    *blocks, mine_ref, other_ref, cross_ref = refs
    a, b = both_blocks(blocks)
    n = a.shape[1]
    a_hi, a_lo = split(jnp.transpose(a))
    b_hi, b_lo = split(b)
    wide = jnp.dot(a_hi, jnp.concatenate([b_hi, b_lo], 1), preferred_element_type=F32)
    cross = wide[:, :n] + wide[:, n:] + jnp.dot(a_lo, b_hi, preferred_element_type=F32)
    message(
        jnp.sum(a * a, 0, keepdims=True),
        jnp.sum(b * b, 0, keepdims=True),
        cross,
        core_ref[0],
        cross_ref,
        mine_ref,
        other_ref,
    )


def cayley_blocks(core_ref, mine_ref, other_ref):
    half = mine_ref.shape[0] - PAD
    first = core_ref[0] == 0
    mine = mine_ref[...]
    other = other_ref[...]
    low = jnp.where(first, mine, other)
    high = jnp.where(first, other, mine)
    cross = jnp.concatenate([low[:half], high[:half]], 0)
    return rotation(cross, low[half : half + 1], high[half : half + 1])


def rows_times(rows, top, low):
    x_hi, x_lo = rows
    n = top.shape[1]
    c_hi, c_lo = split(jnp.concatenate([top, low], 0))
    wide = jnp.dot(x_hi, jnp.concatenate([c_hi, c_lo], 1), preferred_element_type=F32)
    return wide[:, :n] + wide[:, n:] + jnp.dot(x_lo, c_hi, preferred_element_type=F32)


def first_kernel(core_ref, mine_ref, other_ref, *refs):
    *blocks, a_out = refs
    c11, _, c21, _ = cayley_blocks(core_ref, mine_ref, other_ref)
    rows = split(jnp.concatenate(both_blocks(blocks), 1))
    a_out[...] = rows_times(rows, c11, c21)


def both_kernel(core_ref, mine_ref, other_ref, *refs):
    *blocks, a_out, b_out = refs
    c11, c12, c21, c22 = cayley_blocks(core_ref, mine_ref, other_ref)
    rows = split(jnp.concatenate(both_blocks(blocks), 1))
    b_out[...] = rows_times(rows, c12, c22)
    a_out[...] = rows_times(rows, c11, c21)


def last_kernel(core_ref, mine_ref, other_ref, *refs):
    own_ref, *blocks, out_ref, b_ref, sems = refs
    n = own_ref.shape[1]
    own_copy = pltpu.make_async_copy(own_ref, out_ref.at[:, :n], sems.at[0])
    own_copy.start()
    _, c12, _, c22 = cayley_blocks(core_ref, mine_ref, other_ref)
    rows = split(jnp.concatenate(both_blocks(blocks), 1))
    b_ref[...] = rows_times(rows, c12, c22)
    b_copy = pltpu.make_async_copy(b_ref, out_ref.at[:, n:], sems.at[1])
    b_copy.start()
    own_copy.wait()
    b_copy.wait()


def in_specs(count):
    return [pl.BlockSpec(memory_space=pltpu.SMEM)] + [
        pl.BlockSpec(memory_space=pltpu.VMEM)
    ] * count


def near(x):
    return pltpu.with_memory_space_constraint(x, pltpu.VMEM)


def gram(core, blocks, n):
    half = pltpu.VMEM((n // 2 + PAD, n), F32)
    return pl.pallas_call(
        gram_kernel,
        out_shape=[half, half],
        in_specs=in_specs(len(blocks)),
        scratch_shapes=[pltpu.VMEM((n + 2 * PAD, n), F32)],
        name="gram",
    )(core, *map(near, blocks))


def turn_first(core, halves, blocks, n):
    return pl.pallas_call(
        first_kernel,
        out_shape=pltpu.VMEM((blocks[0].shape[0], n), F32),
        in_specs=in_specs(2 + len(blocks)),
        name="turn_first",
    )(core, *map(near, halves), *map(near, blocks))


def turn_both(core, halves, blocks, n):
    return pl.pallas_call(
        both_kernel,
        out_shape=[pltpu.VMEM((blocks[0].shape[0], n), F32)] * 2,
        in_specs=in_specs(2 + len(blocks)),
        name="turn_both",
    )(core, *map(near, halves), *map(near, blocks))


def turn_last(core, halves, own, blocks):
    rows, n = own.shape
    return pl.pallas_call(
        last_kernel,
        out_shape=jax.ShapeDtypeStruct((rows, 2 * n), F32),
        in_specs=in_specs(3 + len(blocks)),
        out_specs=pl.BlockSpec(memory_space=pl.ANY),
        scratch_shapes=[pltpu.VMEM((rows, n), F32), pltpu.SemaphoreType.DMA((2,))],
        name="turn_last",
    )(core, *map(near, halves), near(own), *map(near, blocks))


def from_row(x, source):
    devices = range(lax.axis_size("row"))
    line = len(devices) // QUAD
    route = []
    for i in devices:
        z, y_lo, core = source(i // QUAD, i // 2 % 2, i % 2)
        route.append((z % line * QUAD + y_lo * 2 + core, i))
    return lax.ppermute(x, "row", route)


def side(z):
    return 1 if z % 2 else -1


def summed_halves(mine, other):
    x = mine + from_row(other, lambda z, y, c: (z, y, 1 - c))
    x = (
        (x + from_row(x, lambda z, y, c: (z ^ 1, y, c)))
        + from_row(x, lambda z, y, c: (z, 1 - y, c))
        + from_row(x, lambda z, y, c: (z ^ 1, 1 - y, c))
    )
    x = (
        (x + from_row(x, lambda z, y, c: (z + side(z), y, c)))
        + from_row(x, lambda z, y, c: (z - 2 * side(z), y, c))
        + from_row(x, lambda z, y, c: (z + 3 * side(z), y, c))
    )
    return x


def with_other(half):
    return [half, from_row(half, lambda z, y, c: (z, y, 1 - c))]


def shifted(block):
    devices = range(lax.axis_size("pair"))
    route = [((i - 1) % len(devices), i) for i in devices]
    return lax.ppermute(block, "pair", route)


def local(panel):
    n = panel.shape[1] // 2
    core = (lax.axis_index("row") & 1).astype(jnp.int32).reshape(1)
    own = [panel]
    before = [shifted(panel)]
    for step in range(STEPS):
        mine, other = gram(core, own, n)
        half = summed_halves(mine, other)
        hopped = shifted(half)
        a = turn_first(core, with_other(half), own, n)
        halves = with_other(hopped)
        if step + 1 == STEPS:
            return turn_last(core, halves, a, before)
        a_before, b = turn_both(core, halves, before, n)
        own = [a, b]
        before = [a_before, shifted(b)]


def solution(mesh):
    return jax.shard_map(
        local,
        mesh=mesh,
        in_specs=(P("row", "pair"),),
        out_specs=P("row", "pair"),
        check_vma=False,
    )
```

```python
import jax
import jax.numpy as jnp
from jax import lax
from jax.experimental import pallas as pl
from jax.experimental.pallas import tpu as pltpu
from jax.sharding import PartitionSpec as P


STEPS = 3

BF16 = jnp.bfloat16
F32 = jnp.float32
HIGH = lax.Precision.HIGHEST

QUAD = 4
PAD = 8
CHUNKS = 4


def split(x):
    hi = x.astype(BF16)
    return hi, (x - hi.astype(F32)).astype(BF16)


def left3(x):
    return jnp.concatenate(split(x), 1)


def right3(x):
    hi, lo = split(x)
    top = jnp.concatenate([hi, lo], 1)
    low = jnp.concatenate([hi, jnp.zeros_like(hi)], 1)
    return jnp.concatenate([top, low], 0)


def times3(left, right):
    out = jnp.dot(left, right, preferred_element_type=F32)
    n = out.shape[1] // 2
    return out[:, :n] + out[:, n:]


def times(a, b):
    return jnp.dot(a, b, precision=HIGH, preferred_element_type=F32)


def rotation(cross, diag_a, diag_b):
    n = cross.shape[0]
    scale_a = lax.rsqrt(diag_a + 1e-06)
    scale_b = lax.rsqrt(diag_b + 1e-06)
    d = 0.25 * (cross * jnp.transpose(jnp.broadcast_to(scale_a, (n, n))) * scale_b)
    dt = jnp.transpose(d)
    shape = (n, n)
    eye = jnp.where(
        lax.broadcasted_iota(jnp.int32, shape, 0) == lax.broadcasted_iota(jnp.int32, shape, 1),
        1.0,
        0.0,
    ).astype(F32)
    base = eye + times(d, dt)
    top = 1.0 + 1.001 * (0.25 * n) ** 2
    start = 2.0 / (1.0 + top)
    gap = (top - 1.0) / (top + 1.0)
    y = start * base
    x = None
    while gap > 0.05:
        z = 2.0 * eye - y
        stretch = 2.0 / (2.0 - gap * gap)
        right = right3(z)
        if x is None:
            y = stretch * times3(left3(y), right)
            x = (stretch * start) * z
        else:
            both = stretch * times3(jnp.concatenate([left3(x), left3(y)], 0), right)
            x, y = both[:n], both[n:]
        gap = gap * gap / (2.0 - gap * gap)
    left = eye - times3(left3(x), right3(base))
    x = x + times3(left3(left), right3(x))
    left = eye - times(x, base)
    x = x + times3(left3(left), right3(x))
    md = times(x, d)
    mixed = 2.0 * md
    corner = eye - 2.0 * times3(left3(dt), right3(md))
    return 2.0 * x - eye, mixed, -jnp.transpose(mixed), corner


def message(diag_a, diag_b, cross, core, cross_ref, mine_ref, other_ref):
    n = cross.shape[0]
    half = n // 2
    step = half + PAD
    cross_ref[:half] = cross[:half]
    cross_ref[step : step + half] = cross[half:]
    cross_ref[half:step] = jnp.broadcast_to(diag_a, (PAD, n))
    cross_ref[step + half :] = jnp.broadcast_to(diag_b, (PAD, n))
    mine_ref[...] = cross_ref[pl.ds(pl.multiple_of(core * step, 8), step), :]
    other_ref[...] = cross_ref[pl.ds(pl.multiple_of((1 - core) * step, 8), step), :]


def both_blocks(refs):
    if len(refs) == 1:
        n = refs[0].shape[1] // 2
        return refs[0][:, :n], refs[0][:, n:]
    return refs[0][...], refs[1][...]


def gram_kernel(core_ref, *refs):
    *blocks, mine_ref, other_ref, cross_ref = refs
    a, b = both_blocks(blocks)
    n = a.shape[1]
    a_hi, a_lo = split(jnp.transpose(a))
    b_hi, b_lo = split(b)
    wide = jnp.dot(a_hi, jnp.concatenate([b_hi, b_lo], 1), preferred_element_type=F32)
    cross = wide[:, :n] + wide[:, n:] + jnp.dot(a_lo, b_hi, preferred_element_type=F32)
    message(
        jnp.sum(a * a, 0, keepdims=True),
        jnp.sum(b * b, 0, keepdims=True),
        cross,
        core_ref[0],
        cross_ref,
        mine_ref,
        other_ref,
    )


def cayley_blocks(core_ref, mine_ref, other_ref):
    half = mine_ref.shape[0] - PAD
    first = core_ref[0] == 0
    mine = mine_ref[...]
    other = other_ref[...]
    low = jnp.where(first, mine, other)
    high = jnp.where(first, other, mine)
    cross = jnp.concatenate([low[:half], high[:half]], 0)
    return rotation(cross, low[half : half + 1], high[half : half + 1])


def rows_times(rows, top, low):
    x_hi, x_lo = rows
    n = top.shape[1]
    c_hi, c_lo = split(jnp.concatenate([top, low], 0))
    wide = jnp.dot(x_hi, jnp.concatenate([c_hi, c_lo], 1), preferred_element_type=F32)
    return wide[:, :n] + wide[:, n:] + jnp.dot(x_lo, c_hi, preferred_element_type=F32)


def first_kernel(core_ref, mine_ref, other_ref, *refs):
    *blocks, a_out = refs
    c11, _, c21, _ = cayley_blocks(core_ref, mine_ref, other_ref)
    rows = split(jnp.concatenate(both_blocks(blocks), 1))
    a_out[...] = rows_times(rows, c11, c21)


def both_kernel(core_ref, mine_ref, other_ref, *refs):
    *blocks, a_out, b_out = refs
    c11, c12, c21, c22 = cayley_blocks(core_ref, mine_ref, other_ref)
    rows = split(jnp.concatenate(both_blocks(blocks), 1))
    b_out[...] = rows_times(rows, c12, c22)
    a_out[...] = rows_times(rows, c11, c21)


def last_kernel(core_ref, mine_ref, other_ref, *refs):
    own_ref, *blocks, out_ref, b_ref, sems = refs
    rows, n = own_ref.shape
    copies = [pltpu.make_async_copy(own_ref, out_ref.at[:, :n], sems.at[CHUNKS])]
    copies[0].start()
    _, c12, _, c22 = cayley_blocks(core_ref, mine_ref, other_ref)
    both = jnp.concatenate(both_blocks(blocks), 1)
    size = rows // CHUNKS
    for i in range(CHUNKS):
        part = slice(i * size, (i + 1) * size)
        b_ref[part] = rows_times(split(both[part]), c12, c22)
        copy = pltpu.make_async_copy(b_ref.at[part], out_ref.at[part, n:], sems.at[i])
        copy.start()
        copies.append(copy)
    for copy in copies:
        copy.wait()


def in_specs(count):
    return [pl.BlockSpec(memory_space=pltpu.SMEM)] + [
        pl.BlockSpec(memory_space=pltpu.VMEM)
    ] * count


def near(x):
    return pltpu.with_memory_space_constraint(x, pltpu.VMEM)


def gram(core, blocks, n):
    half = pltpu.VMEM((n // 2 + PAD, n), F32)
    return pl.pallas_call(
        gram_kernel,
        out_shape=[half, half],
        in_specs=in_specs(len(blocks)),
        scratch_shapes=[pltpu.VMEM((n + 2 * PAD, n), F32)],
        name="gram",
    )(core, *map(near, blocks))


def turn_first(core, halves, blocks, n):
    return pl.pallas_call(
        first_kernel,
        out_shape=pltpu.VMEM((blocks[0].shape[0], n), F32),
        in_specs=in_specs(2 + len(blocks)),
        name="turn_first",
    )(core, *map(near, halves), *map(near, blocks))


def turn_both(core, halves, blocks, n):
    return pl.pallas_call(
        both_kernel,
        out_shape=[pltpu.VMEM((blocks[0].shape[0], n), F32)] * 2,
        in_specs=in_specs(2 + len(blocks)),
        name="turn_both",
    )(core, *map(near, halves), *map(near, blocks))


def turn_last(core, halves, own, blocks):
    rows, n = own.shape
    return pl.pallas_call(
        last_kernel,
        out_shape=jax.ShapeDtypeStruct((rows, 2 * n), F32),
        in_specs=in_specs(3 + len(blocks)),
        out_specs=pl.BlockSpec(memory_space=pl.ANY),
        scratch_shapes=[pltpu.VMEM((rows, n), F32), pltpu.SemaphoreType.DMA((CHUNKS + 1,))],
        name="turn_last",
    )(core, *map(near, halves), near(own), *map(near, blocks))


def from_row(x, source):
    devices = range(lax.axis_size("row"))
    line = len(devices) // QUAD
    route = []
    for i in devices:
        z, y_lo, core = source(i // QUAD, i // 2 % 2, i % 2)
        route.append((z % line * QUAD + y_lo * 2 + core, i))
    return lax.ppermute(x, "row", route)


def side(z):
    return 1 if z % 2 else -1


def summed_halves(mine, other, y_last):
    x = mine + from_row(other, lambda z, y, c: (z, y, 1 - c))
    if y_last:
        x = x + from_row(x, lambda z, y, c: (z ^ 1, y, c))
    else:
        x = (
            (x + from_row(x, lambda z, y, c: (z ^ 1, y, c)))
            + from_row(x, lambda z, y, c: (z, 1 - y, c))
            + from_row(x, lambda z, y, c: (z ^ 1, 1 - y, c))
        )
    x = (
        (x + from_row(x, lambda z, y, c: (z + side(z), y, c)))
        + from_row(x, lambda z, y, c: (z - 2 * side(z), y, c))
        + from_row(x, lambda z, y, c: (z + 3 * side(z), y, c))
    )
    if y_last:
        x = x + from_row(x, lambda z, y, c: (z, 1 - y, c))
    return x


def with_other(half):
    return [half, from_row(half, lambda z, y, c: (z, y, 1 - c))]


def shifted(block):
    devices = range(lax.axis_size("pair"))
    route = [((i - 1) % len(devices), i) for i in devices]
    return lax.ppermute(block, "pair", route)


def local(panel):
    n = panel.shape[1] // 2
    core = (lax.axis_index("row") & 1).astype(jnp.int32).reshape(1)
    own = [panel]
    for step in range(STEPS):
        if step == 0:
            before = [shifted(panel)]
        mine, other = gram(core, own, n)
        half = summed_halves(mine, other, y_last=step == 0)
        hopped = shifted(half)
        a = turn_first(core, with_other(half), own, n)
        halves = with_other(hopped)
        if step + 1 == STEPS:
            return turn_last(core, halves, a, before)
        a_before, b = turn_both(core, halves, before, n)
        own = [a, b]
        before = [a_before, shifted(b)]


def solution(mesh):
    return jax.shard_map(
        local,
        mesh=mesh,
        in_specs=(P("row", "pair"),),
        out_specs=P("row", "pair"),
        check_vma=False,
    )
```

```python
import jax
import jax.numpy as jnp
from jax import lax
from jax.experimental import pallas as pl
from jax.experimental.pallas import tpu as pltpu
from jax.sharding import PartitionSpec as P


STEPS = 3

BF16 = jnp.bfloat16
F32 = jnp.float32
HIGH = lax.Precision.HIGHEST

QUAD = 4
PAD = 8
CHUNKS = 4


def split(x):
    hi = x.astype(BF16)
    return hi, (x - hi.astype(F32)).astype(BF16)


def left3(x):
    return jnp.concatenate(split(x), 1)


def right3(x):
    hi, lo = split(x)
    top = jnp.concatenate([hi, lo], 1)
    low = jnp.concatenate([hi, jnp.zeros_like(hi)], 1)
    return jnp.concatenate([top, low], 0)


def times3(left, right):
    out = jnp.dot(left, right, preferred_element_type=F32)
    n = out.shape[1] // 2
    return out[:, :n] + out[:, n:]


def times(a, b):
    return jnp.dot(a, b, precision=HIGH, preferred_element_type=F32)


def rotation(cross, diag_a, diag_b):
    n = cross.shape[0]
    scale_a = lax.rsqrt(diag_a + 1e-06)
    scale_b = lax.rsqrt(diag_b + 1e-06)
    d = 0.25 * (cross * jnp.transpose(jnp.broadcast_to(scale_a, (n, n))) * scale_b)
    dt = jnp.transpose(d)
    shape = (n, n)
    eye = jnp.where(
        lax.broadcasted_iota(jnp.int32, shape, 0) == lax.broadcasted_iota(jnp.int32, shape, 1),
        1.0,
        0.0,
    ).astype(F32)
    base = eye + times(d, dt)
    top = 1.0 + 1.001 * (0.25 * n) ** 2
    start = 2.0 / (1.0 + top)
    gap = (top - 1.0) / (top + 1.0)
    y = start * base
    x = None
    while gap > 0.05:
        z = 2.0 * eye - y
        stretch = 2.0 / (2.0 - gap * gap)
        right = right3(z)
        if x is None:
            y = stretch * times3(left3(y), right)
            x = (stretch * start) * z
        else:
            both = stretch * times3(jnp.concatenate([left3(x), left3(y)], 0), right)
            x, y = both[:n], both[n:]
        gap = gap * gap / (2.0 - gap * gap)
    left = eye - times3(left3(x), right3(base))
    x = x + times3(left3(left), right3(x))
    left = eye - times(x, base)
    x = x + times3(left3(left), right3(x))
    md = times(x, d)
    mixed = 2.0 * md
    corner = eye - 2.0 * times3(left3(dt), right3(md))
    return 2.0 * x - eye, mixed, -jnp.transpose(mixed), corner


def message(diag_a, diag_b, cross, core, cross_ref, mine_ref, other_ref):
    n = cross.shape[0]
    half = n // 2
    step = half + PAD
    cross_ref[:half] = cross[:half]
    cross_ref[step : step + half] = cross[half:]
    cross_ref[half:step] = jnp.broadcast_to(diag_a, (PAD, n))
    cross_ref[step + half :] = jnp.broadcast_to(diag_b, (PAD, n))
    mine_ref[...] = cross_ref[pl.ds(pl.multiple_of(core * step, 8), step), :]
    other_ref[...] = cross_ref[pl.ds(pl.multiple_of((1 - core) * step, 8), step), :]


def both_blocks(refs):
    if len(refs) == 1:
        n = refs[0].shape[1] // 2
        return refs[0][:, :n], refs[0][:, n:]
    return refs[0][...], refs[1][...]


def gram_kernel(core_ref, *refs):
    *blocks, mine_ref, other_ref, cross_ref = refs
    a, b = both_blocks(blocks)
    n = a.shape[1]
    a_hi, a_lo = split(jnp.transpose(a))
    b_hi, b_lo = split(b)
    wide = jnp.dot(a_hi, jnp.concatenate([b_hi, b_lo], 1), preferred_element_type=F32)
    cross = wide[:, :n] + wide[:, n:] + jnp.dot(a_lo, b_hi, preferred_element_type=F32)
    message(
        jnp.sum(a * a, 0, keepdims=True),
        jnp.sum(b * b, 0, keepdims=True),
        cross,
        core_ref[0],
        cross_ref,
        mine_ref,
        other_ref,
    )


def cayley_blocks(core_ref, mine_ref, other_ref):
    half = mine_ref.shape[0] - PAD
    first = core_ref[0] == 0
    mine = mine_ref[...]
    other = other_ref[...]
    low = jnp.where(first, mine, other)
    high = jnp.where(first, other, mine)
    cross = jnp.concatenate([low[:half], high[:half]], 0)
    return rotation(cross, low[half : half + 1], high[half : half + 1])


def rows_times(rows, top, low):
    x_hi, x_lo = rows
    n = top.shape[1]
    c_hi, c_lo = split(jnp.concatenate([top, low], 0))
    wide = jnp.dot(x_hi, jnp.concatenate([c_hi, c_lo], 1), preferred_element_type=F32)
    return wide[:, :n] + wide[:, n:] + jnp.dot(x_lo, c_hi, preferred_element_type=F32)


def first_kernel(core_ref, mine_ref, other_ref, *refs):
    *blocks, a_out = refs
    c11, _, c21, _ = cayley_blocks(core_ref, mine_ref, other_ref)
    rows = split(jnp.concatenate(both_blocks(blocks), 1))
    a_out[...] = rows_times(rows, c11, c21)


def both_kernel(core_ref, mine_ref, other_ref, *refs):
    *blocks, a_out, b_out = refs
    c11, c12, c21, c22 = cayley_blocks(core_ref, mine_ref, other_ref)
    rows = split(jnp.concatenate(both_blocks(blocks), 1))
    b_out[...] = rows_times(rows, c12, c22)
    a_out[...] = rows_times(rows, c11, c21)


def last_kernel(core_ref, mine_ref, other_ref, *refs):
    own_ref, *blocks, out_ref, b_ref, sems = refs
    rows, n = own_ref.shape
    copies = [pltpu.make_async_copy(own_ref, out_ref.at[:, :n], sems.at[CHUNKS])]
    copies[0].start()
    _, c12, _, c22 = cayley_blocks(core_ref, mine_ref, other_ref)
    both = jnp.concatenate(both_blocks(blocks), 1)
    size = rows // CHUNKS
    for i in range(CHUNKS):
        part = slice(i * size, (i + 1) * size)
        b_ref[part] = rows_times(split(both[part]), c12, c22)
        copy = pltpu.make_async_copy(b_ref.at[part], out_ref.at[part, n:], sems.at[i])
        copy.start()
        copies.append(copy)
    for copy in copies:
        copy.wait()


def in_specs(count):
    return [pl.BlockSpec(memory_space=pltpu.SMEM)] + [
        pl.BlockSpec(memory_space=pltpu.VMEM)
    ] * count


def near(x):
    return pltpu.with_memory_space_constraint(x, pltpu.VMEM)


def gram(core, blocks, n):
    half = pltpu.VMEM((n // 2 + PAD, n), F32)
    return pl.pallas_call(
        gram_kernel,
        out_shape=[half, half],
        in_specs=in_specs(len(blocks)),
        scratch_shapes=[pltpu.VMEM((n + 2 * PAD, n), F32)],
        name="gram",
    )(core, *map(near, blocks))


def turn_first(core, halves, blocks, n):
    return pl.pallas_call(
        first_kernel,
        out_shape=pltpu.VMEM((blocks[0].shape[0], n), F32),
        in_specs=in_specs(2 + len(blocks)),
        name="turn_first",
    )(core, *map(near, halves), *map(near, blocks))


def turn_both(core, halves, blocks, n):
    return pl.pallas_call(
        both_kernel,
        out_shape=[pltpu.VMEM((blocks[0].shape[0], n), F32)] * 2,
        in_specs=in_specs(2 + len(blocks)),
        name="turn_both",
    )(core, *map(near, halves), *map(near, blocks))


def turn_last(core, halves, own, blocks):
    rows, n = own.shape
    return pl.pallas_call(
        last_kernel,
        out_shape=jax.ShapeDtypeStruct((rows, 2 * n), F32),
        in_specs=in_specs(3 + len(blocks)),
        out_specs=pl.BlockSpec(memory_space=pl.ANY),
        scratch_shapes=[pltpu.VMEM((rows, n), F32), pltpu.SemaphoreType.DMA((CHUNKS + 1,))],
        name="turn_last",
    )(core, *map(near, halves), near(own), *map(near, blocks))


def from_row(x, source):
    devices = range(lax.axis_size("row"))
    line = len(devices) // QUAD
    route = []
    for i in devices:
        z, y_lo, core = source(i // QUAD, i // 2 % 2, i % 2)
        route.append((z % line * QUAD + y_lo * 2 + core, i))
    return lax.ppermute(x, "row", route)


def side(z):
    return 1 if z % 2 else -1


def summed_halves(mine, other, y_last):
    mate = from_row(other, lambda z, y, c: (z, y, 1 - c))
    x = mine + mate
    next_z = from_row(x, lambda z, y, c: (z ^ 1, y, c))
    if y_last:
        x = x + next_z
    else:
        next_y = from_row(x, lambda z, y, c: (z, 1 - y, c))
        next_zy = from_row(x, lambda z, y, c: (z ^ 1, 1 - y, c))
        x = ((x + next_z) + next_y) + next_zy
    x = (
        (x + from_row(x, lambda z, y, c: (z + side(z), y, c)))
        + from_row(x, lambda z, y, c: (z - 2 * side(z), y, c))
        + from_row(x, lambda z, y, c: (z + 3 * side(z), y, c))
    )
    if y_last:
        x = x + from_row(x, lambda z, y, c: (z, 1 - y, c))
    return x


def with_other(half):
    return [half, from_row(half, lambda z, y, c: (z, y, 1 - c))]


def shifted(block):
    devices = range(lax.axis_size("pair"))
    route = [((i - 1) % len(devices), i) for i in devices]
    return lax.ppermute(block, "pair", route)


def local(panel):
    n = panel.shape[1] // 2
    core = (lax.axis_index("row") & 1).astype(jnp.int32).reshape(1)
    own = [panel]
    for step in range(STEPS):
        if step == 0:
            before = [shifted(panel)]
        else:
            before = [a_before, shifted(own[1])]
        mine, other = gram(core, own, n)
        half = summed_halves(mine, other, y_last=step == 0)
        hopped = shifted(half)
        own_halves = with_other(half)
        a = turn_first(core, own_halves, own, n)
        halves = with_other(hopped)
        if step + 1 == STEPS:
            return turn_last(core, halves, a, before)
        a_before, b = turn_both(core, halves, before, n)
        own = [a, b]


def solution(mesh):
    return jax.shard_map(
        local,
        mesh=mesh,
        in_specs=(P("row", "pair"),),
        out_specs=P("row", "pair"),
        check_vma=False,
    )
```

```python
import jax
import jax.numpy as jnp
from jax import lax
from jax.experimental import pallas as pl
from jax.experimental.pallas import tpu as pltpu
from jax.sharding import PartitionSpec as P


STEPS = 3

BF16 = jnp.bfloat16
F32 = jnp.float32
HIGH = lax.Precision.HIGHEST

QUAD = 4
PAD = 8
CHUNKS = 4


def split(x):
    hi = x.astype(BF16)
    return hi, (x - hi.astype(F32)).astype(BF16)


def left3(x):
    return jnp.concatenate(split(x), 1)


def right3(x):
    hi, lo = split(x)
    top = jnp.concatenate([hi, lo], 1)
    low = jnp.concatenate([hi, jnp.zeros_like(hi)], 1)
    return jnp.concatenate([top, low], 0)


def times3(left, right):
    out = jnp.dot(left, right, preferred_element_type=F32)
    n = out.shape[1] // 2
    return out[:, :n] + out[:, n:]


def times(a, b):
    return jnp.dot(a, b, precision=HIGH, preferred_element_type=F32)


def quarter_cosines(cross, diag_a, diag_b):
    shape = cross.shape
    scale_a = lax.rsqrt(diag_a + 1e-06)
    scale_b = lax.rsqrt(diag_b + 1e-06)
    return 0.25 * (cross * jnp.transpose(jnp.broadcast_to(scale_a, shape)) * scale_b)


def damped_inverse(d, dt):
    n = d.shape[0]
    shape = (n, n)
    eye = jnp.where(
        lax.broadcasted_iota(jnp.int32, shape, 0) == lax.broadcasted_iota(jnp.int32, shape, 1),
        1.0,
        0.0,
    ).astype(F32)
    base = eye + times(d, dt)
    top = 1.0 + 1.001 * (0.25 * n) ** 2
    start = 2.0 / (1.0 + top)
    gap = (top - 1.0) / (top + 1.0)
    y = start * base
    x = None
    while gap > 0.05:
        z = 2.0 * eye - y
        stretch = 2.0 / (2.0 - gap * gap)
        right = right3(z)
        if x is None:
            y = stretch * times3(left3(y), right)
            x = (stretch * start) * z
        else:
            both = stretch * times3(jnp.concatenate([left3(x), left3(y)], 0), right)
            x, y = both[:n], both[n:]
        gap = gap * gap / (2.0 - gap * gap)
    left = eye - times3(left3(x), right3(base))
    x = x + times3(left3(left), right3(x))
    wide = times(x, jnp.concatenate([base, d], 1))
    left = eye - wide[:, :n]
    both = jnp.concatenate([x, wide[:, n:]], 1)
    both = both + times3(left3(left), right3(both))
    return both[:, :n], both[:, n:]


def message(diag_a, diag_b, cross, core, cross_ref, mine_ref, other_ref):
    n = cross.shape[0]
    half = n // 2
    step = half + PAD
    cross_ref[:half] = cross[:half]
    cross_ref[step : step + half] = cross[half:]
    cross_ref[half:step] = jnp.broadcast_to(diag_a, (PAD, n))
    cross_ref[step + half :] = jnp.broadcast_to(diag_b, (PAD, n))
    mine_ref[...] = cross_ref[pl.ds(pl.multiple_of(core * step, 8), step), :]
    other_ref[...] = cross_ref[pl.ds(pl.multiple_of((1 - core) * step, 8), step), :]


def both_blocks(refs):
    if len(refs) == 1:
        n = refs[0].shape[1] // 2
        return refs[0][:, :n], refs[0][:, n:]
    return refs[0][...], refs[1][...]


def cross_of(a, b):
    n = a.shape[1]
    a_hi, a_lo = split(jnp.transpose(a))
    b_hi, b_lo = split(b)
    wide = jnp.dot(a_hi, jnp.concatenate([b_hi, b_lo], 1), preferred_element_type=F32)
    return wide[:, :n] + wide[:, n:] + jnp.dot(a_lo, b_hi, preferred_element_type=F32)


def squares(block):
    return jnp.sum(block * block, 0, keepdims=True)


def gram_kernel(core_ref, *refs):
    *blocks, mine_ref, other_ref, cross_ref = refs
    a, b = both_blocks(blocks)
    message(squares(a), squares(b), cross_of(a, b), core_ref[0], cross_ref, mine_ref, other_ref)


def cosines_of(core_ref, mine_ref, other_ref):
    half = mine_ref.shape[0] - PAD
    first = core_ref[0] == 0
    mine = mine_ref[...]
    other = other_ref[...]
    low = jnp.where(first, mine, other)
    high = jnp.where(first, other, mine)
    cross = jnp.concatenate([low[:half], high[:half]], 0)
    return quarter_cosines(cross, low[half : half + 1], high[half : half + 1])


def first_block(a, b, m, md):
    n = m.shape[0]
    x_hi, x_lo = split(jnp.concatenate([a, b], 1))
    c_hi, c_lo = split(jnp.concatenate([m, -jnp.transpose(md)], 0))
    wide = jnp.dot(x_hi, jnp.concatenate([c_hi, c_lo], 1), preferred_element_type=F32)
    low = jnp.dot(x_lo, c_hi, preferred_element_type=F32)
    return 2.0 * (wide[:, :n] + wide[:, n:] + low) - a


def first_kernel(core_ref, mine_ref, other_ref, *refs):
    *blocks, a_out = refs
    d = cosines_of(core_ref, mine_ref, other_ref)
    a, b = both_blocks(blocks)
    a_out[...] = first_block(a, b, *damped_inverse(d, jnp.transpose(d)))


def late_kernel(m_ref, md_ref, *refs):
    *blocks, a_out = refs
    a, b = both_blocks(blocks)
    a_out[...] = first_block(a, b, m_ref[...], md_ref[...])


def second_kernel(core_ref, mine_ref, other_ref, own_ref, *refs):
    *blocks, b_out, m_out, md_out, mine_out, other_out, cross_ref = refs
    d = cosines_of(core_ref, mine_ref, other_ref)
    dt = jnp.transpose(d)
    a, b = both_blocks(blocks)
    turned = left3(a - times3(left3(b), right3(dt)))
    own = own_ref[...]
    m, md = damped_inverse(d, dt)
    b = b + 2.0 * times3(turned, right3(md))
    message(
        squares(own), squares(b), cross_of(own, b), core_ref[0], cross_ref, mine_out, other_out
    )
    b_out[...] = b
    m_out[...] = m
    md_out[...] = md


def last_kernel(core_ref, mine_ref, other_ref, own_ref, *refs):
    *blocks, out_ref, b_ref, sems = refs
    rows, n = own_ref.shape
    copies = [pltpu.make_async_copy(own_ref, out_ref.at[:, :n], sems.at[CHUNKS])]
    copies[0].start()
    d = cosines_of(core_ref, mine_ref, other_ref)
    dt = jnp.transpose(d)
    a, b = both_blocks(blocks)
    turned = left3(a - times3(left3(b), right3(dt)))
    _, md = damped_inverse(d, dt)
    right = right3(md)
    size = rows // CHUNKS
    for i in range(CHUNKS):
        part = slice(i * size, (i + 1) * size)
        b_ref[part] = b[part] + 2.0 * times3(turned[part], right)
        copy = pltpu.make_async_copy(b_ref.at[part], out_ref.at[part, n:], sems.at[i])
        copy.start()
        copies.append(copy)
    for copy in copies:
        copy.wait()


def near(x):
    return pltpu.with_memory_space_constraint(x, pltpu.VMEM)


def vmem_call(kernel, shapes, arrays, core=None, scratch=(), **options):
    specs = [pl.BlockSpec(memory_space=pltpu.VMEM)] * len(arrays)
    arrays = [near(x) for x in arrays]
    if core is not None:
        specs = [pl.BlockSpec(memory_space=pltpu.SMEM)] + specs
        arrays = [core] + arrays
    return pl.pallas_call(
        kernel, out_shape=shapes, in_specs=specs, scratch_shapes=scratch, **options
    )(*arrays)


def message_shapes(n):
    half = pltpu.VMEM((n // 2 + PAD, n), F32)
    return [half, half], [pltpu.VMEM((n + 2 * PAD, n), F32)]


def gram(core, blocks, n):
    halves, scratch = message_shapes(n)
    return vmem_call(gram_kernel, halves, blocks, core, scratch)


def turn_first(core, halves, blocks, n):
    block = pltpu.VMEM((blocks[0].shape[0], n), F32)
    return vmem_call(first_kernel, block, [*halves, *blocks], core)


def turn_late(m, md, blocks, n):
    block = pltpu.VMEM((blocks[0].shape[0], n), F32)
    return vmem_call(late_kernel, block, [m, md, *blocks])


def turn_second(core, halves, own, blocks, n):
    message_out, scratch = message_shapes(n)
    square = pltpu.VMEM((n, n), F32)
    shapes = [pltpu.VMEM(own.shape, F32), square, square, *message_out]
    arrays = [*halves, own, *blocks]
    return vmem_call(second_kernel, shapes, arrays, core, scratch)


def turn_last(core, halves, own, blocks):
    rows, n = own.shape
    return vmem_call(
        last_kernel,
        jax.ShapeDtypeStruct((rows, 2 * n), F32),
        [*halves, own, *blocks],
        core,
        [pltpu.VMEM((rows, n), F32), pltpu.SemaphoreType.DMA((CHUNKS + 1,))],
        out_specs=pl.BlockSpec(memory_space=pl.ANY),
    )


def from_row(x, source):
    devices = range(lax.axis_size("row"))
    line = len(devices) // QUAD
    route = []
    for i in devices:
        z, y_lo, core = source(i // QUAD, i // 2 % 2, i % 2)
        route.append((z % line * QUAD + y_lo * 2 + core, i))
    return lax.ppermute(x, "row", route)


def side(z):
    return 1 if z % 2 else -1


def summed_halves(mine, other, y_last):
    mate = from_row(other, lambda z, y, c: (z, y, 1 - c))
    x = mine + mate
    next_z = from_row(x, lambda z, y, c: (z ^ 1, y, c))
    if y_last:
        x = x + next_z
    else:
        next_y = from_row(x, lambda z, y, c: (z, 1 - y, c))
        next_zy = from_row(x, lambda z, y, c: (z ^ 1, 1 - y, c))
        x = ((x + next_z) + next_y) + next_zy
    by_one = from_row(x, lambda z, y, c: (z + side(z), y, c))
    by_two = from_row(x, lambda z, y, c: (z - 2 * side(z), y, c))
    by_three = from_row(x, lambda z, y, c: (z + 3 * side(z), y, c))
    x = ((x + by_one) + by_two) + by_three
    if y_last:
        x = x + from_row(x, lambda z, y, c: (z, 1 - y, c))
    return x


def with_other(half):
    return [half, from_row(half, lambda z, y, c: (z, y, 1 - c))]


def shifted(block):
    devices = range(lax.axis_size("pair"))
    route = [((i - 1) % len(devices), i) for i in devices]
    return lax.ppermute(block, "pair", route)


def local(panel):
    n = panel.shape[1] // 2
    core = (lax.axis_index("row") & 1).astype(jnp.int32).reshape(1)
    own = [panel]
    for step in range(STEPS):
        if step == 0:
            before = [shifted(panel)]
            mine, other = gram(core, own, n)
        else:
            second = shifted(b)
            before = [turn_late(m, md, before, n), second]
        half = summed_halves(mine, other, y_last=step == 0)
        hopped = shifted(half)
        own_halves = with_other(half)
        a = turn_first(core, own_halves, own, n)
        halves = with_other(hopped)
        if step + 1 == STEPS:
            return turn_last(core, halves, a, before)
        b, m, md, mine, other = turn_second(core, halves, a, before, n)
        own = [a, b]


def solution(mesh):
    return jax.shard_map(
        local,
        mesh=mesh,
        in_specs=(P("row", "pair"),),
        out_specs=P("row", "pair"),
        check_vma=False,
    )
```

```python
import jax
import jax.numpy as jnp
from jax import lax
from jax.experimental import pallas as pl
from jax.experimental.pallas import tpu as pltpu
from jax.sharding import PartitionSpec as P


STEPS = 3

BF16 = jnp.bfloat16
F32 = jnp.float32
HIGH = lax.Precision.HIGHEST

QUAD = 4
PAD = 8
CHUNKS = 4


def split(x):
    hi = x.astype(BF16)
    return hi, (x - hi.astype(F32)).astype(BF16)


def left3(x):
    return jnp.concatenate(split(x), 1)


def right3(x):
    hi, lo = split(x)
    top = jnp.concatenate([hi, lo], 1)
    low = jnp.concatenate([hi, jnp.zeros_like(hi)], 1)
    return jnp.concatenate([top, low], 0)


def times3(left, right):
    out = jnp.dot(left, right, preferred_element_type=F32)
    n = out.shape[1] // 2
    return out[:, :n] + out[:, n:]


def times(a, b):
    return jnp.dot(a, b, precision=HIGH, preferred_element_type=F32)


def quarter_cosines(cross, diag_a, diag_b):
    shape = cross.shape
    scale_a = lax.rsqrt(diag_a + 1e-06)
    scale_b = lax.rsqrt(diag_b + 1e-06)
    return 0.25 * (cross * jnp.transpose(jnp.broadcast_to(scale_a, shape)) * scale_b)


def identity(n):
    row = lax.broadcasted_iota(jnp.int32, (n, n), 0)
    column = lax.broadcasted_iota(jnp.int32, (n, n), 1)
    return jnp.where(row == column, 1.0, 0.0).astype(F32)


def rough_inverse(d, dt):
    n = d.shape[0]
    eye = identity(n)
    base = eye + times(d, dt)
    top = 1.0 + 1.001 * (0.25 * n) ** 2
    start = 2.0 / (1.0 + top)
    gap = (top - 1.0) / (top + 1.0)
    y = start * base
    x = None
    while gap > 0.05:
        z = 2.0 * eye - y
        stretch = 2.0 / (2.0 - gap * gap)
        right = right3(z)
        if x is None:
            y = stretch * times3(left3(y), right)
            x = (stretch * start) * z
        else:
            both = stretch * times3(jnp.concatenate([left3(x), left3(y)], 0), right)
            x, y = both[:n], both[n:]
        gap = gap * gap / (2.0 - gap * gap)
    left = eye - times3(left3(x), right3(base))
    x = x + times3(left3(left), right3(x))
    return base, x


def corrected(base, x, d):
    n = d.shape[0]
    wide = times(x, jnp.concatenate([base, d], 1))
    left = identity(n) - wide[:, :n]
    both = jnp.concatenate([x, wide[:, n:]], 1)
    both = both + times3(left3(left), right3(both))
    return both[:, :n], both[:, n:]


def message(diag_a, diag_b, cross, core, cross_ref, mine_ref, other_ref):
    n = cross.shape[0]
    half = n // 2
    step = half + PAD
    cross_ref[:half] = cross[:half]
    cross_ref[step : step + half] = cross[half:]
    cross_ref[half:step] = jnp.broadcast_to(diag_a, (PAD, n))
    cross_ref[step + half :] = jnp.broadcast_to(diag_b, (PAD, n))
    mine_ref[...] = cross_ref[pl.ds(pl.multiple_of(core * step, 8), step), :]
    other_ref[...] = cross_ref[pl.ds(pl.multiple_of((1 - core) * step, 8), step), :]


def both_blocks(refs):
    if len(refs) == 1:
        n = refs[0].shape[1] // 2
        return refs[0][:, :n], refs[0][:, n:]
    return refs[0][...], refs[1][...]


def cross_of(a, b):
    n = a.shape[1]
    a_hi, a_lo = split(jnp.transpose(a))
    b_hi, b_lo = split(b)
    wide = jnp.dot(a_hi, jnp.concatenate([b_hi, b_lo], 1), preferred_element_type=F32)
    return wide[:, :n] + wide[:, n:] + jnp.dot(a_lo, b_hi, preferred_element_type=F32)


def squares(block):
    return jnp.sum(block * block, 0, keepdims=True)


def load_kernel(core_ref, panel_ref, near_ref, mine_ref, other_ref, cross_ref, sems):
    rows, n = near_ref.shape[0], near_ref.shape[1] // 2
    size = rows // CHUNKS
    parts = [slice(i * size, (i + 1) * size) for i in range(CHUNKS)]
    copies = [
        pltpu.make_async_copy(panel_ref.at[part], near_ref.at[part], sems.at[i])
        for i, part in enumerate(parts)
    ]
    for copy in copies:
        copy.start()
    sums = []
    for copy, part in zip(copies, parts):
        copy.wait()
        a, b = near_ref[part, :n], near_ref[part, n:]
        sums.append((squares(a), squares(b), cross_of(a, b)))
    diag_a, diag_b, cross = (sum(terms[1:], terms[0]) for terms in zip(*sums))
    message(diag_a, diag_b, cross, core_ref[0], cross_ref, mine_ref, other_ref)


def cosines_of(core_ref, mine_ref, other_ref):
    half = mine_ref.shape[0] - PAD
    first = core_ref[0] == 0
    mine = mine_ref[...]
    other = other_ref[...]
    low = jnp.where(first, mine, other)
    high = jnp.where(first, other, mine)
    cross = jnp.concatenate([low[:half], high[:half]], 0)
    return quarter_cosines(cross, low[half : half + 1], high[half : half + 1])


def first_block(a, b, m, md):
    n = m.shape[0]
    x_hi, x_lo = split(jnp.concatenate([a, b], 1))
    c_hi, c_lo = split(jnp.concatenate([m, -jnp.transpose(md)], 0))
    wide = jnp.dot(x_hi, jnp.concatenate([c_hi, c_lo], 1), preferred_element_type=F32)
    low = jnp.dot(x_lo, c_hi, preferred_element_type=F32)
    return 2.0 * (wide[:, :n] + wide[:, n:] + low) - a


def head_kernel(core_ref, mine_ref, other_ref, base_out, x_out, d_out):
    d = cosines_of(core_ref, mine_ref, other_ref)
    d_out[...] = d
    base_out[...], x_out[...] = rough_inverse(d, jnp.transpose(d))


def tail_kernel(base_ref, x_ref, d_ref, *refs):
    *blocks, a_out = refs
    a, b = both_blocks(blocks)
    a_out[...] = first_block(a, b, *corrected(base_ref[...], x_ref[...], d_ref[...]))


def late_kernel(m_ref, md_ref, *refs):
    *blocks, a_out = refs
    a, b = both_blocks(blocks)
    a_out[...] = first_block(a, b, m_ref[...], md_ref[...])


def second_kernel(core_ref, mine_ref, other_ref, own_ref, *refs):
    *blocks, b_out, m_out, md_out, mine_out, other_out, cross_ref = refs
    d = cosines_of(core_ref, mine_ref, other_ref)
    dt = jnp.transpose(d)
    a, b = both_blocks(blocks)
    turned = left3(a - times3(left3(b), right3(dt)))
    own = own_ref[...]
    m, md = corrected(*rough_inverse(d, dt), d)
    b = b + 2.0 * times3(turned, right3(md))
    message(
        squares(own), squares(b), cross_of(own, b), core_ref[0], cross_ref, mine_out, other_out
    )
    b_out[...] = b
    m_out[...] = m
    md_out[...] = md


def last_kernel(core_ref, mine_ref, other_ref, own_ref, *refs):
    *blocks, out_ref, b_ref, sems = refs
    rows, n = own_ref.shape
    copies = [pltpu.make_async_copy(own_ref, out_ref.at[:, :n], sems.at[CHUNKS])]
    copies[0].start()
    d = cosines_of(core_ref, mine_ref, other_ref)
    dt = jnp.transpose(d)
    a, b = both_blocks(blocks)
    turned = left3(a - times3(left3(b), right3(dt)))
    _, md = corrected(*rough_inverse(d, dt), d)
    right = right3(md)
    size = rows // CHUNKS
    for i in range(CHUNKS):
        part = slice(i * size, (i + 1) * size)
        b_ref[part] = b[part] + 2.0 * times3(turned[part], right)
        copy = pltpu.make_async_copy(b_ref.at[part], out_ref.at[part, n:], sems.at[i])
        copy.start()
        copies.append(copy)
    for copy in copies:
        copy.wait()


def near(x):
    return pltpu.with_memory_space_constraint(x, pltpu.VMEM)


def vmem_call(kernel, shapes, arrays, core=None, scratch=(), **options):
    specs = [pl.BlockSpec(memory_space=pltpu.VMEM)] * len(arrays)
    arrays = [near(x) for x in arrays]
    if core is not None:
        specs = [pl.BlockSpec(memory_space=pltpu.SMEM)] + specs
        arrays = [core] + arrays
    return pl.pallas_call(
        kernel, out_shape=shapes, in_specs=specs, scratch_shapes=scratch, **options
    )(*arrays)


def message_shapes(n):
    half = pltpu.VMEM((n // 2 + PAD, n), F32)
    return [half, half], [pltpu.VMEM((n + 2 * PAD, n), F32)]


def load(core, panel, n):
    halves, scratch = message_shapes(n)
    return pl.pallas_call(
        load_kernel,
        out_shape=[pltpu.VMEM(panel.shape, F32), *halves],
        in_specs=[pl.BlockSpec(memory_space=pltpu.SMEM), pl.BlockSpec(memory_space=pl.ANY)],
        scratch_shapes=[*scratch, pltpu.SemaphoreType.DMA((CHUNKS,))],
        name="load",
    )(core, panel)


def turn_head(core, halves, n):
    squares = [pltpu.VMEM((n, n), F32)] * 3
    return vmem_call(head_kernel, squares, halves, core)


def turn_tail(squares, blocks, n):
    block = pltpu.VMEM((blocks[0].shape[0], n), F32)
    return vmem_call(tail_kernel, block, [*squares, *blocks])


def turn_late(m, md, blocks, n):
    block = pltpu.VMEM((blocks[0].shape[0], n), F32)
    return vmem_call(late_kernel, block, [m, md, *blocks])


def turn_second(core, halves, own, blocks, n):
    message_out, scratch = message_shapes(n)
    square = pltpu.VMEM((n, n), F32)
    shapes = [pltpu.VMEM(own.shape, F32), square, square, *message_out]
    arrays = [*halves, own, *blocks]
    return vmem_call(second_kernel, shapes, arrays, core, scratch)


def turn_last(core, halves, own, blocks):
    rows, n = own.shape
    return vmem_call(
        last_kernel,
        jax.ShapeDtypeStruct((rows, 2 * n), F32),
        [*halves, own, *blocks],
        core,
        [pltpu.VMEM((rows, n), F32), pltpu.SemaphoreType.DMA((CHUNKS + 1,))],
        out_specs=pl.BlockSpec(memory_space=pl.ANY),
    )


def from_row(x, source):
    devices = range(lax.axis_size("row"))
    line = len(devices) // QUAD
    route = []
    for i in devices:
        z, y_lo, core = source(i // QUAD, i // 2 % 2, i % 2)
        route.append((z % line * QUAD + y_lo * 2 + core, i))
    return lax.ppermute(x, "row", route)


def side(z):
    return 1 if z % 2 else -1


def summed_halves(mine, other, y_last):
    mate = from_row(other, lambda z, y, c: (z, y, 1 - c))
    x = mine + mate
    next_z = from_row(x, lambda z, y, c: (z ^ 1, y, c))
    if y_last:
        x = x + next_z
    else:
        next_y = from_row(x, lambda z, y, c: (z, 1 - y, c))
        next_zy = from_row(x, lambda z, y, c: (z ^ 1, 1 - y, c))
        x = ((x + next_z) + next_y) + next_zy
    by_one = from_row(x, lambda z, y, c: (z + side(z), y, c))
    by_two = from_row(x, lambda z, y, c: (z - 2 * side(z), y, c))
    by_three = from_row(x, lambda z, y, c: (z + 3 * side(z), y, c))
    x = ((x + by_one) + by_two) + by_three
    if y_last:
        x = x + from_row(x, lambda z, y, c: (z, 1 - y, c))
    return x


def with_other(half):
    return [half, from_row(half, lambda z, y, c: (z, y, 1 - c))]


def shifted(block):
    devices = range(lax.axis_size("pair"))
    route = [((i - 1) % len(devices), i) for i in devices]
    return lax.ppermute(block, "pair", route)


def local(panel):
    n = panel.shape[1] // 2
    core = (lax.axis_index("row") & 1).astype(jnp.int32).reshape(1)
    for step in range(STEPS):
        if step == 0:
            before = [shifted(panel)]
            own, mine, other = load(core, panel, n)
            own = [own]
        else:
            second = shifted(b)
            before = [turn_late(m, md, before, n), second]
        half = summed_halves(mine, other, y_last=step == 0)
        hopped = shifted(half)
        own_halves = with_other(half)
        squares = turn_head(core, own_halves, n)
        halves = with_other(hopped)
        a = turn_tail(squares, own, n)
        if step + 1 == STEPS:
            return turn_last(core, halves, a, before)
        b, m, md, mine, other = turn_second(core, halves, a, before, n)
        own = [a, b]


def solution(mesh):
    return jax.shard_map(
        local,
        mesh=mesh,
        in_specs=(P("row", "pair"),),
        out_specs=P("row", "pair"),
        check_vma=False,
    )
```

```python
import jax
import jax.numpy as jnp
from jax import lax
from jax.experimental import pallas as pl
from jax.experimental.pallas import tpu as pltpu
from jax.sharding import PartitionSpec as P


STEPS = 3

BF16 = jnp.bfloat16
F32 = jnp.float32
HIGH = lax.Precision.HIGHEST

QUAD = 4
PAD = 8
CHUNKS = 4


def split(x):
    hi = x.astype(BF16)
    return hi, (x - hi.astype(F32)).astype(BF16)


def left3(x):
    return jnp.concatenate(split(x), 1)


def right3(x):
    hi, lo = split(x)
    top = jnp.concatenate([hi, lo], 1)
    low = jnp.concatenate([hi, jnp.zeros_like(hi)], 1)
    return jnp.concatenate([top, low], 0)


def times3(left, right):
    out = jnp.dot(left, right, preferred_element_type=F32)
    n = out.shape[1] // 2
    return out[:, :n] + out[:, n:]


def times(a, b):
    return jnp.dot(a, b, precision=HIGH, preferred_element_type=F32)


def quarter_cosines(cross, diag_a, diag_b):
    shape = cross.shape
    scale_a = lax.rsqrt(diag_a + 1e-06)
    scale_b = lax.rsqrt(diag_b + 1e-06)
    return 0.25 * (cross * jnp.transpose(jnp.broadcast_to(scale_a, shape)) * scale_b)


def identity(n):
    row = lax.broadcasted_iota(jnp.int32, (n, n), 0)
    column = lax.broadcasted_iota(jnp.int32, (n, n), 1)
    return jnp.where(row == column, 1.0, 0.0).astype(F32)


def rough_inverse(d, dt):
    n = d.shape[0]
    eye = identity(n)
    base = eye + times(d, dt)
    top = 1.0 + 1.001 * (0.25 * n) ** 2
    start = 2.0 / (1.0 + top)
    gap = (top - 1.0) / (top + 1.0)
    y = start * base
    x = None
    while gap > 0.05:
        z = 2.0 * eye - y
        stretch = 2.0 / (2.0 - gap * gap)
        right = right3(z)
        if x is None:
            y = stretch * times3(left3(y), right)
            x = (stretch * start) * z
        else:
            both = stretch * times3(jnp.concatenate([left3(x), left3(y)], 0), right)
            x, y = both[:n], both[n:]
        gap = gap * gap / (2.0 - gap * gap)
    left = eye - times3(left3(x), right3(base))
    x = x + times3(left3(left), right3(x))
    return base, x


def corrected(base, x, d):
    n = d.shape[0]
    wide = times(x, jnp.concatenate([base, d], 1))
    left = identity(n) - wide[:, :n]
    both = jnp.concatenate([x, wide[:, n:]], 1)
    both = both + times3(left3(left), right3(both))
    return both[:, :n], both[:, n:]


def message(diag_a, diag_b, cross, core, cross_ref, mine_ref, other_ref):
    n = cross.shape[0]
    half = n // 2
    step = half + PAD
    cross_ref[:half] = cross[:half]
    cross_ref[step : step + half] = cross[half:]
    cross_ref[half:step] = jnp.broadcast_to(diag_a, (PAD, n))
    cross_ref[step + half :] = jnp.broadcast_to(diag_b, (PAD, n))
    mine_ref[...] = cross_ref[pl.ds(pl.multiple_of(core * step, 8), step), :]
    other_ref[...] = cross_ref[pl.ds(pl.multiple_of((1 - core) * step, 8), step), :]


def both_blocks(refs):
    if len(refs) == 1:
        n = refs[0].shape[1] // 2
        return refs[0][:, :n], refs[0][:, n:]
    return refs[0][...], refs[1][...]


def cross_of(a, b):
    n = a.shape[1]
    a_hi, a_lo = split(jnp.transpose(a))
    b_hi, b_lo = split(b)
    wide = jnp.dot(a_hi, jnp.concatenate([b_hi, b_lo], 1), preferred_element_type=F32)
    return wide[:, :n] + wide[:, n:] + jnp.dot(a_lo, b_hi, preferred_element_type=F32)


def squares(block):
    return jnp.sum(block * block, 0, keepdims=True)


def load_kernel(core_ref, panel_ref, near_ref, mine_ref, other_ref, cross_ref, sem):
    copy = pltpu.make_async_copy(panel_ref, near_ref, sem)
    copy.start()
    copy.wait()
    a, b = both_blocks([near_ref])
    message(squares(a), squares(b), cross_of(a, b), core_ref[0], cross_ref, mine_ref, other_ref)


def cosines_of(core_ref, mine_ref, other_ref):
    half = mine_ref.shape[0] - PAD
    first = core_ref[0] == 0
    mine = mine_ref[...]
    other = other_ref[...]
    low = jnp.where(first, mine, other)
    high = jnp.where(first, other, mine)
    cross = jnp.concatenate([low[:half], high[:half]], 0)
    return quarter_cosines(cross, low[half : half + 1], high[half : half + 1])


def first_block(a, b, m, md):
    n = m.shape[0]
    x_hi, x_lo = split(jnp.concatenate([a, b], 1))
    c_hi, c_lo = split(jnp.concatenate([m, -jnp.transpose(md)], 0))
    wide = jnp.dot(x_hi, jnp.concatenate([c_hi, c_lo], 1), preferred_element_type=F32)
    low = jnp.dot(x_lo, c_hi, preferred_element_type=F32)
    return 2.0 * (wide[:, :n] + wide[:, n:] + low) - a


def head_kernel(core_ref, mine_ref, other_ref, base_out, x_out, d_out):
    d = cosines_of(core_ref, mine_ref, other_ref)
    d_out[...] = d
    base_out[...], x_out[...] = rough_inverse(d, jnp.transpose(d))


def tail_kernel(base_ref, x_ref, d_ref, *refs):
    *blocks, a_out = refs
    a, b = both_blocks(blocks)
    a_out[...] = first_block(a, b, *corrected(base_ref[...], x_ref[...], d_ref[...]))


def late_kernel(m_ref, md_ref, *refs):
    *blocks, a_out = refs
    a, b = both_blocks(blocks)
    a_out[...] = first_block(a, b, m_ref[...], md_ref[...])


def second_kernel(core_ref, mine_ref, other_ref, own_ref, *refs):
    *blocks, b_out, m_out, md_out, mine_out, other_out, cross_ref = refs
    d = cosines_of(core_ref, mine_ref, other_ref)
    dt = jnp.transpose(d)
    a, b = both_blocks(blocks)
    turned = left3(a - times3(left3(b), right3(dt)))
    own = own_ref[...]
    m, md = corrected(*rough_inverse(d, dt), d)
    b = b + 2.0 * times3(turned, right3(md))
    message(
        squares(own), squares(b), cross_of(own, b), core_ref[0], cross_ref, mine_out, other_out
    )
    b_out[...] = b
    m_out[...] = m
    md_out[...] = md


def last_kernel(core_ref, mine_ref, other_ref, own_ref, *refs):
    *blocks, out_ref, b_ref, sems = refs
    rows, n = own_ref.shape
    copies = [pltpu.make_async_copy(own_ref, out_ref.at[:, :n], sems.at[CHUNKS])]
    copies[0].start()
    d = cosines_of(core_ref, mine_ref, other_ref)
    dt = jnp.transpose(d)
    a, b = both_blocks(blocks)
    turned = left3(a - times3(left3(b), right3(dt)))
    _, md = corrected(*rough_inverse(d, dt), d)
    right = right3(md)
    size = rows // CHUNKS
    for i in range(CHUNKS):
        part = slice(i * size, (i + 1) * size)
        b_ref[part] = b[part] + 2.0 * times3(turned[part], right)
        copy = pltpu.make_async_copy(b_ref.at[part], out_ref.at[part, n:], sems.at[i])
        copy.start()
        copies.append(copy)
    for copy in copies:
        copy.wait()


def near(x):
    return pltpu.with_memory_space_constraint(x, pltpu.VMEM)


def vmem_call(kernel, shapes, arrays, core=None, scratch=(), **options):
    specs = [pl.BlockSpec(memory_space=pltpu.VMEM)] * len(arrays)
    arrays = [near(x) for x in arrays]
    if core is not None:
        specs = [pl.BlockSpec(memory_space=pltpu.SMEM)] + specs
        arrays = [core] + arrays
    return pl.pallas_call(
        kernel, out_shape=shapes, in_specs=specs, scratch_shapes=scratch, **options
    )(*arrays)


def message_shapes(n):
    half = pltpu.VMEM((n // 2 + PAD, n), F32)
    return [half, half], [pltpu.VMEM((n + 2 * PAD, n), F32)]


def load(core, panel, n):
    halves, scratch = message_shapes(n)
    return pl.pallas_call(
        load_kernel,
        out_shape=[pltpu.VMEM(panel.shape, F32), *halves],
        in_specs=[pl.BlockSpec(memory_space=pltpu.SMEM), pl.BlockSpec(memory_space=pl.ANY)],
        scratch_shapes=[*scratch, pltpu.SemaphoreType.DMA],
        name="load",
    )(core, panel)


def turn_head(core, halves, n):
    squares = [pltpu.VMEM((n, n), F32)] * 3
    return vmem_call(head_kernel, squares, halves, core)


def turn_tail(squares, blocks, n):
    block = pltpu.VMEM((blocks[0].shape[0], n), F32)
    return vmem_call(tail_kernel, block, [*squares, *blocks])


def turn_late(m, md, blocks, n):
    block = pltpu.VMEM((blocks[0].shape[0], n), F32)
    return vmem_call(late_kernel, block, [m, md, *blocks])


def turn_second(core, halves, own, blocks, n):
    message_out, scratch = message_shapes(n)
    square = pltpu.VMEM((n, n), F32)
    shapes = [pltpu.VMEM(own.shape, F32), square, square, *message_out]
    arrays = [*halves, own, *blocks]
    return vmem_call(second_kernel, shapes, arrays, core, scratch)


def turn_last(core, halves, own, blocks):
    rows, n = own.shape
    return vmem_call(
        last_kernel,
        jax.ShapeDtypeStruct((rows, 2 * n), F32),
        [*halves, own, *blocks],
        core,
        [pltpu.VMEM((rows, n), F32), pltpu.SemaphoreType.DMA((CHUNKS + 1,))],
        out_specs=pl.BlockSpec(memory_space=pl.ANY),
    )


def from_row(x, source):
    devices = range(lax.axis_size("row"))
    line = len(devices) // QUAD
    route = []
    for i in devices:
        z, y_lo, core = source(i // QUAD, i // 2 % 2, i % 2)
        route.append((z % line * QUAD + y_lo * 2 + core, i))
    return lax.ppermute(x, "row", route)


def side(z):
    return 1 if z % 2 else -1


def summed_halves(mine, other, y_last):
    mate = from_row(other, lambda z, y, c: (z, y, 1 - c))
    x = mine + mate
    next_z = from_row(x, lambda z, y, c: (z ^ 1, y, c))
    if y_last:
        x = x + next_z
    else:
        next_y = from_row(x, lambda z, y, c: (z, 1 - y, c))
        next_zy = from_row(x, lambda z, y, c: (z ^ 1, 1 - y, c))
        x = ((x + next_z) + next_y) + next_zy
    by_one = from_row(x, lambda z, y, c: (z + side(z), y, c))
    by_two = from_row(x, lambda z, y, c: (z - 2 * side(z), y, c))
    by_three = from_row(x, lambda z, y, c: (z + 3 * side(z), y, c))
    x = ((x + by_one) + by_two) + by_three
    if y_last:
        x = x + from_row(x, lambda z, y, c: (z, 1 - y, c))
    return x


def with_other(half):
    return [half, from_row(half, lambda z, y, c: (z, y, 1 - c))]


def shifted(block):
    devices = range(lax.axis_size("pair"))
    route = [((i - 1) % len(devices), i) for i in devices]
    return lax.ppermute(block, "pair", route)


def local(panel):
    n = panel.shape[1] // 2
    core = (lax.axis_index("row") & 1).astype(jnp.int32).reshape(1)
    for step in range(STEPS):
        if step == 0:
            own, mine, other = load(core, panel, n)
            before = [shifted(own)]
            own = [own]
        else:
            second = shifted(b)
            before = [turn_late(m, md, before, n), second]
        half = summed_halves(mine, other, y_last=step == 0)
        hopped = shifted(half)
        own_halves = with_other(half)
        squares = turn_head(core, own_halves, n)
        halves = with_other(hopped)
        a = turn_tail(squares, own, n)
        if step + 1 == STEPS:
            return turn_last(core, halves, a, before)
        b, m, md, mine, other = turn_second(core, halves, a, before, n)
        own = [a, b]


def solution(mesh):
    return jax.shard_map(
        local,
        mesh=mesh,
        in_specs=(P("row", "pair"),),
        out_specs=P("row", "pair"),
        check_vma=False,
    )
```

```python
import jax
import jax.numpy as jnp
from jax import lax
from jax.experimental import pallas as pl
from jax.experimental.pallas import tpu as pltpu
from jax.sharding import PartitionSpec as P


STEPS = 3

BF16 = jnp.bfloat16
F32 = jnp.float32
HIGH = lax.Precision.HIGHEST

QUAD = 4
PAD = 8
CHUNKS = 4


def split(x):
    hi = x.astype(BF16)
    return hi, (x - hi.astype(F32)).astype(BF16)


def left3(x):
    return jnp.concatenate(split(x), 1)


def right3(x):
    hi, lo = split(x)
    top = jnp.concatenate([hi, lo], 1)
    low = jnp.concatenate([hi, jnp.zeros_like(hi)], 1)
    return jnp.concatenate([top, low], 0)


def times3(left, right):
    out = jnp.dot(left, right, preferred_element_type=F32)
    n = out.shape[1] // 2
    return out[:, :n] + out[:, n:]


def times(a, b):
    return jnp.dot(a, b, precision=HIGH, preferred_element_type=F32)


def quarter_cosines(cross, diag_a, diag_b):
    shape = cross.shape
    scale_a = lax.rsqrt(diag_a + 1e-06)
    scale_b = lax.rsqrt(diag_b + 1e-06)
    return 0.25 * (cross * jnp.transpose(jnp.broadcast_to(scale_a, shape)) * scale_b)


def identity(n):
    row = lax.broadcasted_iota(jnp.int32, (n, n), 0)
    column = lax.broadcasted_iota(jnp.int32, (n, n), 1)
    return jnp.where(row == column, 1.0, 0.0).astype(F32)


def rough_inverse(d, dt):
    n = d.shape[0]
    eye = identity(n)
    base = eye + times(d, dt)
    top = 1.0 + 1.001 * (0.25 * n) ** 2
    start = 2.0 / (1.0 + top)
    gap = (top - 1.0) / (top + 1.0)
    y = start * base
    x = None
    while gap > 0.05:
        z = 2.0 * eye - y
        stretch = 2.0 / (2.0 - gap * gap)
        right = right3(z)
        if x is None:
            y = stretch * times3(left3(y), right)
            x = (stretch * start) * z
        else:
            both = stretch * times3(jnp.concatenate([left3(x), left3(y)], 0), right)
            x, y = both[:n], both[n:]
        gap = gap * gap / (2.0 - gap * gap)
    left = eye - times3(left3(x), right3(base))
    x = x + times3(left3(left), right3(x))
    return base, x


def corrected(base, x, d):
    n = d.shape[0]
    wide = times(x, jnp.concatenate([base, d], 1))
    left = identity(n) - wide[:, :n]
    both = jnp.concatenate([x, wide[:, n:]], 1)
    both = both + times3(left3(left), right3(both))
    return both[:, :n], both[:, n:]


def message(diag_a, diag_b, cross, core, cross_ref, mine_ref, other_ref):
    n = cross.shape[0]
    half = n // 2
    step = half + PAD
    cross_ref[:half] = cross[:half]
    cross_ref[step : step + half] = cross[half:]
    cross_ref[half:step] = jnp.broadcast_to(diag_a, (PAD, n))
    cross_ref[step + half :] = jnp.broadcast_to(diag_b, (PAD, n))
    mine_ref[...] = cross_ref[pl.ds(pl.multiple_of(core * step, 8), step), :]
    other_ref[...] = cross_ref[pl.ds(pl.multiple_of((1 - core) * step, 8), step), :]


def both_blocks(refs):
    if len(refs) == 1:
        n = refs[0].shape[1] // 2
        return refs[0][:, :n], refs[0][:, n:]
    return refs[0][...], refs[1][...]


def cross_of(a, b):
    n = a.shape[1]
    a_hi, a_lo = split(jnp.transpose(a))
    b_hi, b_lo = split(b)
    wide = jnp.dot(a_hi, jnp.concatenate([b_hi, b_lo], 1), preferred_element_type=F32)
    return wide[:, :n] + wide[:, n:] + jnp.dot(a_lo, b_hi, preferred_element_type=F32)


def squares(block):
    return jnp.sum(block * block, 0, keepdims=True)


def load_kernel(core_ref, panel_ref, near_ref, mine_ref, other_ref, cross_ref, sem):
    copy = pltpu.make_async_copy(panel_ref, near_ref, sem)
    copy.start()
    copy.wait()
    a, b = both_blocks([near_ref])
    message(squares(a), squares(b), cross_of(a, b), core_ref[0], cross_ref, mine_ref, other_ref)


def cosines_of(core_ref, mine_ref, other_ref):
    half = mine_ref.shape[0] - PAD
    first = core_ref[0] == 0
    mine = mine_ref[...]
    other = other_ref[...]
    low = jnp.where(first, mine, other)
    high = jnp.where(first, other, mine)
    cross = jnp.concatenate([low[:half], high[:half]], 0)
    return quarter_cosines(cross, low[half : half + 1], high[half : half + 1])


def first_block(a, b, m, md):
    n = m.shape[0]
    x_hi, x_lo = split(jnp.concatenate([a, b], 1))
    c_hi, c_lo = split(jnp.concatenate([m, -jnp.transpose(md)], 0))
    wide = jnp.dot(x_hi, jnp.concatenate([c_hi, c_lo], 1), preferred_element_type=F32)
    low = jnp.dot(x_lo, c_hi, preferred_element_type=F32)
    return 2.0 * (wide[:, :n] + wide[:, n:] + low) - a


def head_kernel(core_ref, mine_ref, other_ref, base_out, x_out, d_out):
    d = cosines_of(core_ref, mine_ref, other_ref)
    d_out[...] = d
    base_out[...], x_out[...] = rough_inverse(d, jnp.transpose(d))


def tail_kernel(base_ref, x_ref, d_ref, *refs):
    *blocks, a_out = refs
    a, b = both_blocks(blocks)
    a_out[...] = first_block(a, b, *corrected(base_ref[...], x_ref[...], d_ref[...]))


def late_kernel(m_ref, md_ref, *refs):
    *blocks, a_out = refs
    a, b = both_blocks(blocks)
    a_out[...] = first_block(a, b, m_ref[...], md_ref[...])


def second_kernel(core_ref, mine_ref, other_ref, own_ref, *refs):
    *blocks, b_out, m_out, md_out, mine_out, other_out, cross_ref = refs
    d = cosines_of(core_ref, mine_ref, other_ref)
    dt = jnp.transpose(d)
    a, b = both_blocks(blocks)
    turned = left3(a - times3(left3(b), right3(dt)))
    own = own_ref[...]
    m, md = corrected(*rough_inverse(d, dt), d)
    b = b + 2.0 * times3(turned, right3(md))
    message(
        squares(own), squares(b), cross_of(own, b), core_ref[0], cross_ref, mine_out, other_out
    )
    b_out[...] = b
    m_out[...] = m
    md_out[...] = md


def last_kernel(core_ref, mine_ref, other_ref, own_ref, *refs):
    *blocks, out_ref, b_ref, sems = refs
    rows, n = own_ref.shape
    copies = [pltpu.make_async_copy(own_ref, out_ref.at[:, :n], sems.at[CHUNKS])]
    copies[0].start()
    d = cosines_of(core_ref, mine_ref, other_ref)
    dt = jnp.transpose(d)
    a, b = both_blocks(blocks)
    turned = left3(a - times3(left3(b), right3(dt)))
    _, md = corrected(*rough_inverse(d, dt), d)
    right = right3(md)
    size = rows // CHUNKS
    for i in range(CHUNKS):
        part = slice(i * size, (i + 1) * size)
        b_ref[part] = b[part] + 2.0 * times3(turned[part], right)
        copy = pltpu.make_async_copy(b_ref.at[part], out_ref.at[part, n:], sems.at[i])
        copy.start()
        copies.append(copy)
    for copy in copies:
        copy.wait()


def near(x):
    return pltpu.with_memory_space_constraint(x, pltpu.VMEM)


def vmem_call(kernel, shapes, arrays, core=None, scratch=(), **options):
    specs = [pl.BlockSpec(memory_space=pltpu.VMEM)] * len(arrays)
    arrays = [near(x) for x in arrays]
    if core is not None:
        specs = [pl.BlockSpec(memory_space=pltpu.SMEM)] + specs
        arrays = [core] + arrays
    return pl.pallas_call(
        kernel, out_shape=shapes, in_specs=specs, scratch_shapes=scratch, **options
    )(*arrays)


def message_shapes(n):
    half = pltpu.VMEM((n // 2 + PAD, n), F32)
    return [half, half], [pltpu.VMEM((n + 2 * PAD, n), F32)]


def load(core, panel, n):
    halves, scratch = message_shapes(n)
    return pl.pallas_call(
        load_kernel,
        out_shape=[pltpu.VMEM(panel.shape, F32), *halves],
        in_specs=[pl.BlockSpec(memory_space=pltpu.SMEM), pl.BlockSpec(memory_space=pl.ANY)],
        scratch_shapes=[*scratch, pltpu.SemaphoreType.DMA],
        name="load",
    )(core, panel)


def turn_head(core, halves, n):
    squares = [pltpu.VMEM((n, n), F32)] * 3
    return vmem_call(head_kernel, squares, halves, core)


def turn_tail(squares, blocks, n):
    block = pltpu.VMEM((blocks[0].shape[0], n), F32)
    return vmem_call(tail_kernel, block, [*squares, *blocks])


def turn_late(m, md, blocks, n):
    block = pltpu.VMEM((blocks[0].shape[0], n), F32)
    return vmem_call(late_kernel, block, [m, md, *blocks])


def turn_second(core, halves, own, blocks, n):
    message_out, scratch = message_shapes(n)
    square = pltpu.VMEM((n, n), F32)
    shapes = [pltpu.VMEM(own.shape, F32), square, square, *message_out]
    arrays = [*halves, own, *blocks]
    return vmem_call(second_kernel, shapes, arrays, core, scratch)


def turn_last(core, halves, own, blocks):
    rows, n = own.shape
    return vmem_call(
        last_kernel,
        jax.ShapeDtypeStruct((rows, 2 * n), F32),
        [*halves, own, *blocks],
        core,
        [pltpu.VMEM((rows, n), F32), pltpu.SemaphoreType.DMA((CHUNKS + 1,))],
        out_specs=pl.BlockSpec(memory_space=pl.ANY),
    )


def from_row(x, source):
    devices = range(lax.axis_size("row"))
    line = len(devices) // QUAD
    route = []
    for i in devices:
        z, y_lo, core = source(i // QUAD, i // 2 % 2, i % 2)
        route.append((z % line * QUAD + y_lo * 2 + core, i))
    return lax.ppermute(x, "row", route)


def mate(z, y, c):
    return z, y, 1 - c


def owner(chip):
    def source(z, y, c):
        other_z, other_y = chip(z, y)
        return other_z, other_y, (c + z + y + other_z + other_y) % 2

    return source


def owned_half(row):
    return (row + row // 2 + row // QUAD) % 2


def side(z):
    return 1 if z % 2 else -1


def summed_halves(mine, other, y_last):
    incoming = from_row(other, mate)
    x = mine + incoming
    next_z = from_row(x, owner(lambda z, y: (z ^ 1, y)))
    if y_last:
        x = x + next_z
    else:
        next_y = from_row(x, owner(lambda z, y: (z, 1 - y)))
        next_zy = from_row(x, owner(lambda z, y: (z ^ 1, 1 - y)))
        x = ((x + next_z) + next_y) + next_zy
    by_one = from_row(x, owner(lambda z, y: (z + side(z), y)))
    by_two = from_row(x, owner(lambda z, y: (z - 2 * side(z), y)))
    by_three = from_row(x, owner(lambda z, y: (z + 3 * side(z), y)))
    x = ((x + by_one) + by_two) + by_three
    if y_last:
        x = x + from_row(x, owner(lambda z, y: (z, 1 - y)))
    return x


def with_other(half):
    return [half, from_row(half, mate)]


def shifted(block):
    devices = range(lax.axis_size("pair"))
    route = [((i - 1) % len(devices), i) for i in devices]
    return lax.ppermute(block, "pair", route)


def local(panel):
    n = panel.shape[1] // 2
    core = owned_half(lax.axis_index("row")).astype(jnp.int32).reshape(1)
    for step in range(STEPS):
        if step == 0:
            own, mine, other = load(core, panel, n)
            before = [shifted(own)]
            own = [own]
        else:
            second = shifted(b)
            before = [turn_late(m, md, before, n), second]
        half = summed_halves(mine, other, y_last=step == 0)
        hopped = shifted(half)
        own_halves = with_other(half)
        squares = turn_head(core, own_halves, n)
        halves = with_other(hopped)
        a = turn_tail(squares, own, n)
        if step + 1 == STEPS:
            return turn_last(core, halves, a, before)
        b, m, md, mine, other = turn_second(core, halves, a, before, n)
        own = [a, b]


def solution(mesh):
    return jax.shard_map(
        local,
        mesh=mesh,
        in_specs=(P("row", "pair"),),
        out_specs=P("row", "pair"),
        check_vma=False,
    )
```

```python
import jax
import jax.numpy as jnp
from jax import lax
from jax.experimental import pallas as pl
from jax.experimental.pallas import tpu as pltpu
from jax.sharding import PartitionSpec as P


STEPS = 3

BF16 = jnp.bfloat16
F32 = jnp.float32
HIGH = lax.Precision.HIGHEST

QUAD = 4
PAD = 8
CHUNKS = 4


def split(x):
    hi = x.astype(BF16)
    return hi, (x - hi.astype(F32)).astype(BF16)


def left3(x):
    return jnp.concatenate(split(x), 1)


def right3(x):
    hi, lo = split(x)
    top = jnp.concatenate([hi, lo], 1)
    low = jnp.concatenate([hi, jnp.zeros_like(hi)], 1)
    return jnp.concatenate([top, low], 0)


def times3(left, right):
    out = jnp.dot(left, right, preferred_element_type=F32)
    n = out.shape[1] // 2
    return out[:, :n] + out[:, n:]


def times(a, b):
    return jnp.dot(a, b, precision=HIGH, preferred_element_type=F32)


def quarter_cosines(cross, diag_a, diag_b):
    shape = cross.shape
    scale_a = lax.rsqrt(diag_a + 1e-06)
    scale_b = lax.rsqrt(diag_b + 1e-06)
    return 0.25 * (cross * jnp.transpose(jnp.broadcast_to(scale_a, shape)) * scale_b)


def identity(n):
    row = lax.broadcasted_iota(jnp.int32, (n, n), 0)
    column = lax.broadcasted_iota(jnp.int32, (n, n), 1)
    return jnp.where(row == column, 1.0, 0.0).astype(F32)


def rough_inverse(d, dt):
    n = d.shape[0]
    eye = identity(n)
    base = eye + times(d, dt)
    top = 1.0 + 1.001 * (0.25 * n) ** 2
    start = 2.0 / (1.0 + top)
    gap = (top - 1.0) / (top + 1.0)
    y = start * base
    x = None
    while gap > 0.05:
        z = 2.0 * eye - y
        stretch = 2.0 / (2.0 - gap * gap)
        right = right3(z)
        if x is None:
            y = stretch * times3(left3(y), right)
            x = (stretch * start) * z
        else:
            both = stretch * times3(jnp.concatenate([left3(x), left3(y)], 0), right)
            x, y = both[:n], both[n:]
        gap = gap * gap / (2.0 - gap * gap)
    left = eye - times3(left3(x), right3(base))
    x = x + times3(left3(left), right3(x))
    return base, x


def corrected(base, x, d):
    n = d.shape[0]
    wide = times(x, jnp.concatenate([base, d], 1))
    left = identity(n) - wide[:, :n]
    both = jnp.concatenate([x, wide[:, n:]], 1)
    both = both + times3(left3(left), right3(both))
    return both[:, :n], both[:, n:]


def message(diag_a, diag_b, cross, core, cross_ref, mine_ref, other_ref):
    n = cross.shape[0]
    half = n // 2
    step = half + PAD
    cross_ref[:half] = cross[:half]
    cross_ref[step : step + half] = cross[half:]
    cross_ref[half:step] = jnp.broadcast_to(diag_a, (PAD, n))
    cross_ref[step + half :] = jnp.broadcast_to(diag_b, (PAD, n))
    mine_ref[...] = cross_ref[pl.ds(pl.multiple_of(core * step, 8), step), :]
    other_ref[...] = cross_ref[pl.ds(pl.multiple_of((1 - core) * step, 8), step), :]


def both_blocks(refs):
    if len(refs) == 1:
        n = refs[0].shape[1] // 2
        return refs[0][:, :n], refs[0][:, n:]
    return refs[0][...], refs[1][...]


def cross_of(a, b):
    n = a.shape[1]
    a_hi, a_lo = split(jnp.transpose(a))
    b_hi, b_lo = split(b)
    wide = jnp.dot(a_hi, jnp.concatenate([b_hi, b_lo], 1), preferred_element_type=F32)
    return wide[:, :n] + wide[:, n:] + jnp.dot(a_lo, b_hi, preferred_element_type=F32)


def squares(block):
    return jnp.sum(block * block, 0, keepdims=True)


def load_kernel(core_ref, panel_ref, near_ref, mine_ref, other_ref, cross_ref, sem):
    copy = pltpu.make_async_copy(panel_ref, near_ref, sem)
    copy.start()
    copy.wait()
    a, b = both_blocks([near_ref])
    message(squares(a), squares(b), cross_of(a, b), core_ref[0], cross_ref, mine_ref, other_ref)


def cosines_of(core_ref, mine_ref, other_ref):
    half = mine_ref.shape[0] - PAD
    first = core_ref[0] == 0
    mine = mine_ref[...]
    other = other_ref[...]
    low = jnp.where(first, mine, other)
    high = jnp.where(first, other, mine)
    cross = jnp.concatenate([low[:half], high[:half]], 0)
    return quarter_cosines(cross, low[half : half + 1], high[half : half + 1])


def first_block(a, b, m, md):
    n = m.shape[0]
    x_hi, x_lo = split(jnp.concatenate([a, b], 1))
    c_hi, c_lo = split(jnp.concatenate([m, -jnp.transpose(md)], 0))
    wide = jnp.dot(x_hi, jnp.concatenate([c_hi, c_lo], 1), preferred_element_type=F32)
    low = jnp.dot(x_lo, c_hi, preferred_element_type=F32)
    return 2.0 * (wide[:, :n] + wide[:, n:] + low) - a


def head_kernel(core_ref, mine_ref, other_ref, base_out, x_out, d_out):
    d = cosines_of(core_ref, mine_ref, other_ref)
    d_out[...] = d
    base_out[...], x_out[...] = rough_inverse(d, jnp.transpose(d))


def tail_kernel(base_ref, x_ref, d_ref, *refs):
    *blocks, a_out = refs
    a, b = both_blocks(blocks)
    a_out[...] = first_block(a, b, *corrected(base_ref[...], x_ref[...], d_ref[...]))


def late_kernel(m_ref, md_ref, *refs):
    *blocks, a_out = refs
    a, b = both_blocks(blocks)
    a_out[...] = first_block(a, b, m_ref[...], md_ref[...])


def second_kernel(core_ref, mine_ref, other_ref, own_ref, *refs):
    *blocks, b_out, m_out, md_out, mine_out, other_out, cross_ref = refs
    d = cosines_of(core_ref, mine_ref, other_ref)
    dt = jnp.transpose(d)
    a, b = both_blocks(blocks)
    turned = left3(a - times3(left3(b), right3(dt)))
    own = own_ref[...]
    m, md = corrected(*rough_inverse(d, dt), d)
    b = b + 2.0 * times3(turned, right3(md))
    message(
        squares(own), squares(b), cross_of(own, b), core_ref[0], cross_ref, mine_out, other_out
    )
    b_out[...] = b
    m_out[...] = m
    md_out[...] = md


def last_kernel(core_ref, mine_ref, other_ref, own_ref, *refs):
    *blocks, out_ref, b_ref, sems = refs
    rows, n = own_ref.shape
    copies = [pltpu.make_async_copy(own_ref, out_ref.at[:, :n], sems.at[CHUNKS])]
    copies[0].start()
    d = cosines_of(core_ref, mine_ref, other_ref)
    dt = jnp.transpose(d)
    a, b = both_blocks(blocks)
    turned = left3(a - times3(left3(b), right3(dt)))
    _, md = corrected(*rough_inverse(d, dt), d)
    right = right3(md)
    size = rows // CHUNKS
    for i in range(CHUNKS):
        part = slice(i * size, (i + 1) * size)
        b_ref[part] = b[part] + 2.0 * times3(turned[part], right)
        copy = pltpu.make_async_copy(b_ref.at[part], out_ref.at[part, n:], sems.at[i])
        copy.start()
        copies.append(copy)
    for copy in copies:
        copy.wait()


def near(x):
    return pltpu.with_memory_space_constraint(x, pltpu.VMEM)


def vmem_call(kernel, shapes, arrays, core=None, scratch=(), **options):
    specs = [pl.BlockSpec(memory_space=pltpu.VMEM)] * len(arrays)
    arrays = [near(x) for x in arrays]
    if core is not None:
        specs = [pl.BlockSpec(memory_space=pltpu.SMEM)] + specs
        arrays = [core] + arrays
    return pl.pallas_call(
        kernel, out_shape=shapes, in_specs=specs, scratch_shapes=scratch, **options
    )(*arrays)


def message_shapes(n):
    half = pltpu.VMEM((n // 2 + PAD, n), F32)
    return [half, half], [pltpu.VMEM((n + 2 * PAD, n), F32)]


def load(core, panel, n):
    halves, scratch = message_shapes(n)
    return pl.pallas_call(
        load_kernel,
        out_shape=[pltpu.VMEM(panel.shape, F32), *halves],
        in_specs=[pl.BlockSpec(memory_space=pltpu.SMEM), pl.BlockSpec(memory_space=pl.ANY)],
        scratch_shapes=[*scratch, pltpu.SemaphoreType.DMA],
        name="load",
    )(core, panel)


def turn_head(core, halves, n):
    squares = [pltpu.VMEM((n, n), F32)] * 3
    return vmem_call(head_kernel, squares, halves, core)


def turn_tail(squares, blocks, n):
    block = pltpu.VMEM((blocks[0].shape[0], n), F32)
    return vmem_call(tail_kernel, block, [*squares, *blocks])


def turn_late(m, md, blocks, n):
    block = pltpu.VMEM((blocks[0].shape[0], n), F32)
    return vmem_call(late_kernel, block, [m, md, *blocks])


def turn_second(core, halves, own, blocks, n):
    message_out, scratch = message_shapes(n)
    square = pltpu.VMEM((n, n), F32)
    shapes = [pltpu.VMEM(own.shape, F32), square, square, *message_out]
    arrays = [*halves, own, *blocks]
    return vmem_call(second_kernel, shapes, arrays, core, scratch)


def turn_last(core, halves, own, blocks):
    rows, n = own.shape
    return vmem_call(
        last_kernel,
        jax.ShapeDtypeStruct((rows, 2 * n), F32),
        [*halves, own, *blocks],
        core,
        [pltpu.VMEM((rows, n), F32), pltpu.SemaphoreType.DMA((CHUNKS + 1,))],
        out_specs=pl.BlockSpec(memory_space=pl.ANY),
    )


def from_row(x, source):
    devices = range(lax.axis_size("row"))
    line = len(devices) // QUAD
    route = []
    for i in devices:
        z, y_lo, core = source(i // QUAD, i // 2 % 2, i % 2)
        route.append((z % line * QUAD + y_lo * 2 + core, i))
    return lax.ppermute(x, "row", route)


def mate(z, y, c):
    return z, y, 1 - c


def owner(chip):
    def source(z, y, c):
        other_z, other_y = chip(z, y)
        return other_z, other_y, (c + z + y + other_z + other_y) % 2

    return source


def side(z):
    return 1 if z % 2 else -1


def summed_halves(mine, other, y_last):
    incoming = from_row(other, mate)
    x = mine + incoming
    next_z = from_row(x, owner(lambda z, y: (z ^ 1, y)))
    if y_last:
        x = x + next_z
    else:
        next_y = from_row(x, owner(lambda z, y: (z, 1 - y)))
        next_zy = from_row(x, owner(lambda z, y: (z ^ 1, 1 - y)))
        x = ((x + next_z) + next_y) + next_zy
    by_one = from_row(x, owner(lambda z, y: (z + side(z), y)))
    by_two = from_row(x, owner(lambda z, y: (z - 2 * side(z), y)))
    by_three = from_row(x, owner(lambda z, y: (z + 3 * side(z), y)))
    x = ((x + by_one) + by_two) + by_three
    if y_last:
        x = x + from_row(x, owner(lambda z, y: (z, 1 - y)))
    return x


def with_other(half):
    return [half, from_row(half, mate)]


def shifted(block):
    devices = range(lax.axis_size("pair"))
    route = [((i - 1) % len(devices), i) for i in devices]
    return lax.ppermute(block, "pair", route)


def local(panel):
    n = panel.shape[1] // 2
    row = lax.axis_index("row")
    core = ((row ^ (row >> 1) ^ (row >> 2)) & 1).astype(jnp.int32).reshape(1)
    for step in range(STEPS):
        if step == 0:
            own, mine, other = load(core, panel, n)
            before = [shifted(own)]
            own = [own]
        else:
            second = shifted(b)
            before = [turn_late(m, md, before, n), second]
        half = summed_halves(mine, other, y_last=step == 0)
        hopped = shifted(half)
        own_halves = with_other(half)
        squares = turn_head(core, own_halves, n)
        halves = with_other(hopped)
        a = turn_tail(squares, own, n)
        if step + 1 == STEPS:
            return turn_last(core, halves, a, before)
        b, m, md, mine, other = turn_second(core, halves, a, before, n)
        own = [a, b]


def solution(mesh):
    return jax.shard_map(
        local,
        mesh=mesh,
        in_specs=(P("row", "pair"),),
        out_specs=P("row", "pair"),
        check_vma=False,
    )
```

```python
import jax
import jax.numpy as jnp
from jax import lax
from jax.experimental import pallas as pl
from jax.experimental.pallas import tpu as pltpu
from jax.sharding import PartitionSpec as P


STEPS = 3

BF16 = jnp.bfloat16
F32 = jnp.float32
HIGH = lax.Precision.HIGHEST

QUAD = 4
PAD = 8
CHUNKS = 4


def split(x):
    hi = x.astype(BF16)
    return hi, (x - hi.astype(F32)).astype(BF16)


def left3(x):
    return jnp.concatenate(split(x), 1)


def right3(x):
    hi, lo = split(x)
    top = jnp.concatenate([hi, lo], 1)
    low = jnp.concatenate([hi, jnp.zeros_like(hi)], 1)
    return jnp.concatenate([top, low], 0)


def times3(left, right):
    out = jnp.dot(left, right, preferred_element_type=F32)
    n = out.shape[1] // 2
    return out[:, :n] + out[:, n:]


def times(a, b):
    return jnp.dot(a, b, precision=HIGH, preferred_element_type=F32)


def quarter_cosines(cross, diag_a, diag_b):
    shape = cross.shape
    scale_a = lax.rsqrt(diag_a + 1e-06)
    scale_b = lax.rsqrt(diag_b + 1e-06)
    return 0.25 * (cross * jnp.transpose(jnp.broadcast_to(scale_a, shape)) * scale_b)


def identity(n):
    row = lax.broadcasted_iota(jnp.int32, (n, n), 0)
    column = lax.broadcasted_iota(jnp.int32, (n, n), 1)
    return jnp.where(row == column, 1.0, 0.0).astype(F32)


def rough_inverse(d, dt):
    n = d.shape[0]
    eye = identity(n)
    base = eye + times(d, dt)
    top = 1.0 + 1.001 * (0.25 * n) ** 2
    start = 2.0 / (1.0 + top)
    gap = (top - 1.0) / (top + 1.0)
    y = start * base
    x = None
    while gap > 0.05:
        z = 2.0 * eye - y
        stretch = 2.0 / (2.0 - gap * gap)
        right = right3(z)
        if x is None:
            y = stretch * times3(left3(y), right)
            x = (stretch * start) * z
        else:
            both = stretch * times3(jnp.concatenate([left3(x), left3(y)], 0), right)
            x, y = both[:n], both[n:]
        gap = gap * gap / (2.0 - gap * gap)
    left = eye - times3(left3(x), right3(base))
    x = x + times3(left3(left), right3(x))
    return base, x


def corrected(base, x, d):
    n = d.shape[0]
    wide = times(x, jnp.concatenate([base, d], 1))
    left = identity(n) - wide[:, :n]
    both = jnp.concatenate([x, wide[:, n:]], 1)
    both = both + times3(left3(left), right3(both))
    return both[:, :n], both[:, n:]


def message(diag_a, diag_b, cross, core, cross_ref, mine_ref, other_ref):
    n = cross.shape[0]
    half = n // 2
    step = half + PAD
    cross_ref[:half] = cross[:half]
    cross_ref[step : step + half] = cross[half:]
    cross_ref[half:step] = jnp.broadcast_to(diag_a, (PAD, n))
    cross_ref[step + half :] = jnp.broadcast_to(diag_b, (PAD, n))
    mine_ref[...] = cross_ref[pl.ds(pl.multiple_of(core * step, 8), step), :]
    other_ref[...] = cross_ref[pl.ds(pl.multiple_of((1 - core) * step, 8), step), :]


def both_blocks(refs):
    if len(refs) == 1:
        n = refs[0].shape[1] // 2
        return refs[0][:, :n], refs[0][:, n:]
    return refs[0][...], refs[1][...]


def cross_of(a, b):
    n = a.shape[1]
    a_hi, a_lo = split(jnp.transpose(a))
    b_hi, b_lo = split(b)
    wide = jnp.dot(a_hi, jnp.concatenate([b_hi, b_lo], 1), preferred_element_type=F32)
    return wide[:, :n] + wide[:, n:] + jnp.dot(a_lo, b_hi, preferred_element_type=F32)


def squares(block):
    return jnp.sum(block * block, 0, keepdims=True)


def load_kernel(core_ref, panel_ref, near_ref, mine_ref, other_ref, cross_ref, sem):
    copy = pltpu.make_async_copy(panel_ref, near_ref, sem)
    copy.start()
    copy.wait()
    a, b = both_blocks([near_ref])
    message(squares(a), squares(b), cross_of(a, b), core_ref[0], cross_ref, mine_ref, other_ref)


def cosines_of(owned, mine_ref, other_ref):
    half = mine_ref.shape[0] - PAD
    first = owned == 0
    mine = mine_ref[...]
    other = other_ref[...]
    low = jnp.where(first, mine, other)
    high = jnp.where(first, other, mine)
    cross = jnp.concatenate([low[:half], high[:half]], 0)
    return quarter_cosines(cross, low[half : half + 1], high[half : half + 1])


def first_block(a, b, m, md):
    n = m.shape[0]
    x_hi, x_lo = split(jnp.concatenate([a, b], 1))
    c_hi, c_lo = split(jnp.concatenate([m, -jnp.transpose(md)], 0))
    wide = jnp.dot(x_hi, jnp.concatenate([c_hi, c_lo], 1), preferred_element_type=F32)
    low = jnp.dot(x_lo, c_hi, preferred_element_type=F32)
    return 2.0 * (wide[:, :n] + wide[:, n:] + low) - a


def head_kernel(core_ref, mine_ref, other_ref, base_out, x_out, d_out):
    d = cosines_of(core_ref[0], mine_ref, other_ref)
    d_out[...] = d
    base_out[...], x_out[...] = rough_inverse(d, jnp.transpose(d))


def tail_kernel(base_ref, x_ref, d_ref, *refs):
    *blocks, a_out = refs
    a, b = both_blocks(blocks)
    a_out[...] = first_block(a, b, *corrected(base_ref[...], x_ref[...], d_ref[...]))


def late_kernel(m_ref, md_ref, *refs):
    *blocks, a_out = refs
    a, b = both_blocks(blocks)
    a_out[...] = first_block(a, b, m_ref[...], md_ref[...])


def second_kernel(core_ref, mine_ref, other_ref, own_ref, *refs):
    *blocks, b_out, m_out, md_out, mine_out, other_out, cross_ref = refs
    d = cosines_of(1 - core_ref[0], mine_ref, other_ref)
    dt = jnp.transpose(d)
    a, b = both_blocks(blocks)
    turned = left3(a - times3(left3(b), right3(dt)))
    own = own_ref[...]
    m, md = corrected(*rough_inverse(d, dt), d)
    b = b + 2.0 * times3(turned, right3(md))
    message(
        squares(own), squares(b), cross_of(own, b), core_ref[0], cross_ref, mine_out, other_out
    )
    b_out[...] = b
    m_out[...] = m
    md_out[...] = md


def last_kernel(core_ref, mine_ref, other_ref, own_ref, *refs):
    *blocks, out_ref, b_ref, sems = refs
    rows, n = own_ref.shape
    copies = [pltpu.make_async_copy(own_ref, out_ref.at[:, :n], sems.at[CHUNKS])]
    copies[0].start()
    d = cosines_of(1 - core_ref[0], mine_ref, other_ref)
    dt = jnp.transpose(d)
    a, b = both_blocks(blocks)
    turned = left3(a - times3(left3(b), right3(dt)))
    _, md = corrected(*rough_inverse(d, dt), d)
    right = right3(md)
    size = rows // CHUNKS
    for i in range(CHUNKS):
        part = slice(i * size, (i + 1) * size)
        b_ref[part] = b[part] + 2.0 * times3(turned[part], right)
        copy = pltpu.make_async_copy(b_ref.at[part], out_ref.at[part, n:], sems.at[i])
        copy.start()
        copies.append(copy)
    for copy in copies:
        copy.wait()


def near(x):
    return pltpu.with_memory_space_constraint(x, pltpu.VMEM)


def vmem_call(kernel, shapes, arrays, core=None, scratch=(), **options):
    specs = [pl.BlockSpec(memory_space=pltpu.VMEM)] * len(arrays)
    arrays = [near(x) for x in arrays]
    if core is not None:
        specs = [pl.BlockSpec(memory_space=pltpu.SMEM)] + specs
        arrays = [core] + arrays
    return pl.pallas_call(
        kernel, out_shape=shapes, in_specs=specs, scratch_shapes=scratch, **options
    )(*arrays)


def message_shapes(n):
    half = pltpu.VMEM((n // 2 + PAD, n), F32)
    return [half, half], [pltpu.VMEM((n + 2 * PAD, n), F32)]


def load(core, panel, n):
    halves, scratch = message_shapes(n)
    return pl.pallas_call(
        load_kernel,
        out_shape=[pltpu.VMEM(panel.shape, F32), *halves],
        in_specs=[pl.BlockSpec(memory_space=pltpu.SMEM), pl.BlockSpec(memory_space=pl.ANY)],
        scratch_shapes=[*scratch, pltpu.SemaphoreType.DMA],
        name="load",
    )(core, panel)


def turn_head(core, halves, n):
    squares = [pltpu.VMEM((n, n), F32)] * 3
    return vmem_call(head_kernel, squares, halves, core)


def turn_tail(squares, blocks, n):
    block = pltpu.VMEM((blocks[0].shape[0], n), F32)
    return vmem_call(tail_kernel, block, [*squares, *blocks])


def turn_late(m, md, blocks, n):
    block = pltpu.VMEM((blocks[0].shape[0], n), F32)
    return vmem_call(late_kernel, block, [m, md, *blocks])


def turn_second(core, halves, own, blocks, n):
    message_out, scratch = message_shapes(n)
    square = pltpu.VMEM((n, n), F32)
    shapes = [pltpu.VMEM(own.shape, F32), square, square, *message_out]
    arrays = [*halves, own, *blocks]
    return vmem_call(second_kernel, shapes, arrays, core, scratch)


def turn_last(core, halves, own, blocks):
    rows, n = own.shape
    return vmem_call(
        last_kernel,
        jax.ShapeDtypeStruct((rows, 2 * n), F32),
        [*halves, own, *blocks],
        core,
        [pltpu.VMEM((rows, n), F32), pltpu.SemaphoreType.DMA((CHUNKS + 1,))],
        out_specs=pl.BlockSpec(memory_space=pl.ANY),
    )


def from_row(x, source):
    devices = range(lax.axis_size("row"))
    line = len(devices) // QUAD
    route = []
    for i in devices:
        z, y_lo, core = source(i // QUAD, i // 2 % 2, i % 2)
        route.append((z % line * QUAD + y_lo * 2 + core, i))
    return lax.ppermute(x, "row", route)


def mate(z, y, c):
    return z, y, 1 - c


def owner(chip):
    def source(z, y, c):
        other_z, other_y = chip(z, y)
        return other_z, other_y, (c + z + y + other_z + other_y) % 2

    return source


def side(z):
    return 1 if z % 2 else -1


def summed_halves(mine, other, y_last):
    incoming = from_row(other, mate)
    x = mine + incoming
    next_z = from_row(x, owner(lambda z, y: (z + side(z), y)))
    if y_last:
        x = x + next_z
    else:
        next_y = from_row(x, owner(lambda z, y: (z, 1 - y)))
        next_zy = from_row(x, owner(lambda z, y: (z + side(z), 1 - y)))
        x = ((x + next_z) + next_y) + next_zy
    by_one = from_row(x, owner(lambda z, y: (z - side(z), y)))
    by_two = from_row(x, owner(lambda z, y: (z + 2 * side(z), y)))
    by_three = from_row(x, owner(lambda z, y: (z - 3 * side(z), y)))
    x = ((x + by_one) + by_two) + by_three
    if y_last:
        x = x + from_row(x, owner(lambda z, y: (z, 1 - y)))
    return x


def with_other(half):
    return [half, from_row(half, mate)]


def shifted(block):
    devices = range(lax.axis_size("pair"))
    route = [((i - 1) % len(devices), i) for i in devices]
    return lax.ppermute(block, "pair", route)


def hopped_over(half):
    pairs = lax.axis_size("pair")
    route = []
    for row in range(lax.axis_size("row")):
        for pair in range(pairs):
            source = (row ^ 1) * pairs + (pair - 1) % pairs
            route.append((source, row * pairs + pair))
    return lax.ppermute(half, ("row", "pair"), route)


def local(panel):
    n = panel.shape[1] // 2
    row = lax.axis_index("row")
    core = ((row ^ (row >> 1) ^ (row >> 2)) & 1).astype(jnp.int32).reshape(1)
    for step in range(STEPS):
        if step == 0:
            own, mine, other = load(core, panel, n)
            before = [shifted(own)]
            own = [own]
        else:
            second = shifted(b)
            before = [turn_late(m, md, before, n), second]
        half = summed_halves(mine, other, y_last=step == 0)
        hopped = hopped_over(half)
        own_halves = with_other(half)
        squares = turn_head(core, own_halves, n)
        halves = with_other(hopped)
        a = turn_tail(squares, own, n)
        if step + 1 == STEPS:
            return turn_last(core, halves, a, before)
        b, m, md, mine, other = turn_second(core, halves, a, before, n)
        own = [a, b]


def solution(mesh):
    return jax.shard_map(
        local,
        mesh=mesh,
        in_specs=(P("row", "pair"),),
        out_specs=P("row", "pair"),
        check_vma=False,
    )
```

```python
import jax
import jax.numpy as jnp
from jax import lax
from jax.experimental import pallas as pl
from jax.experimental.pallas import tpu as pltpu
from jax.sharding import PartitionSpec as P


STEPS = 3

BF16 = jnp.bfloat16
F32 = jnp.float32
HIGH = lax.Precision.HIGHEST

QUAD = 4
PAD = 8
CHUNKS = 4


def split(x):
    hi = x.astype(BF16)
    return hi, (x - hi.astype(F32)).astype(BF16)


def left3(x):
    return jnp.concatenate(split(x), 1)


def right3(x):
    hi, lo = split(x)
    top = jnp.concatenate([hi, lo], 1)
    low = jnp.concatenate([hi, jnp.zeros_like(hi)], 1)
    return jnp.concatenate([top, low], 0)


def times3(left, right):
    out = jnp.dot(left, right, preferred_element_type=F32)
    n = out.shape[1] // 2
    return out[:, :n] + out[:, n:]


def times(a, b):
    return jnp.dot(a, b, precision=HIGH, preferred_element_type=F32)


def quarter_cosines(cross, diag_a, diag_b):
    shape = cross.shape
    scale_a = lax.rsqrt(diag_a + 1e-06)
    scale_b = lax.rsqrt(diag_b + 1e-06)
    return 0.25 * (cross * jnp.transpose(jnp.broadcast_to(scale_a, shape)) * scale_b)


def identity(n):
    row = lax.broadcasted_iota(jnp.int32, (n, n), 0)
    column = lax.broadcasted_iota(jnp.int32, (n, n), 1)
    return jnp.where(row == column, 1.0, 0.0).astype(F32)


def rough_inverse(d, dt):
    n = d.shape[0]
    eye = identity(n)
    base = eye + times(d, dt)
    top = 1.0 + 1.001 * (0.25 * n) ** 2
    start = 2.0 / (1.0 + top)
    gap = (top - 1.0) / (top + 1.0)
    y = start * base
    x = None
    while gap > 0.05:
        z = 2.0 * eye - y
        stretch = 2.0 / (2.0 - gap * gap)
        right = right3(z)
        if x is None:
            y = stretch * times3(left3(y), right)
            x = (stretch * start) * z
        else:
            both = stretch * times3(jnp.concatenate([left3(x), left3(y)], 0), right)
            x, y = both[:n], both[n:]
        gap = gap * gap / (2.0 - gap * gap)
    left = eye - times3(left3(x), right3(base))
    x = x + times3(left3(left), right3(x))
    return base, x


def corrected(base, x, d):
    n = d.shape[0]
    wide = times(x, jnp.concatenate([base, d], 1))
    left = identity(n) - wide[:, :n]
    both = jnp.concatenate([x, wide[:, n:]], 1)
    both = both + times3(left3(left), right3(both))
    return both[:, :n], both[:, n:]


def message(diag_a, diag_b, cross, core, cross_ref, mine_ref, other_ref):
    n = cross.shape[0]
    half = n // 2
    step = half + PAD
    cross_ref[:half] = cross[:half]
    cross_ref[step : step + half] = cross[half:]
    cross_ref[half:step] = jnp.broadcast_to(diag_a, (PAD, n))
    cross_ref[step + half :] = jnp.broadcast_to(diag_b, (PAD, n))
    mine_ref[...] = cross_ref[pl.ds(pl.multiple_of(core * step, 8), step), :]
    other_ref[...] = cross_ref[pl.ds(pl.multiple_of((1 - core) * step, 8), step), :]


def both_blocks(refs):
    if len(refs) == 1:
        n = refs[0].shape[1] // 2
        return refs[0][:, :n], refs[0][:, n:]
    return refs[0][...], refs[1][...]


def cross_of(a, b):
    n = a.shape[1]
    a_hi, a_lo = split(jnp.transpose(a))
    b_hi, b_lo = split(b)
    wide = jnp.dot(a_hi, jnp.concatenate([b_hi, b_lo], 1), preferred_element_type=F32)
    return wide[:, :n] + wide[:, n:] + jnp.dot(a_lo, b_hi, preferred_element_type=F32)


def squares(block):
    return jnp.sum(block * block, 0, keepdims=True)


def load_kernel(core_ref, panel_ref, near_ref, mine_ref, other_ref, cross_ref, sem):
    copy = pltpu.make_async_copy(panel_ref, near_ref, sem)
    copy.start()
    copy.wait()
    a, b = both_blocks([near_ref])
    message(squares(a), squares(b), cross_of(a, b), core_ref[0], cross_ref, mine_ref, other_ref)


def cosines_of(owned, mine_ref, other_ref):
    half = mine_ref.shape[0] - PAD
    first = owned == 0
    mine = mine_ref[...]
    other = other_ref[...]
    low = jnp.where(first, mine, other)
    high = jnp.where(first, other, mine)
    cross = jnp.concatenate([low[:half], high[:half]], 0)
    return quarter_cosines(cross, low[half : half + 1], high[half : half + 1])


def first_block(a, b, m, md):
    n = m.shape[0]
    x_hi, x_lo = split(jnp.concatenate([a, b], 1))
    c_hi, c_lo = split(jnp.concatenate([m, -jnp.transpose(md)], 0))
    wide = jnp.dot(x_hi, jnp.concatenate([c_hi, c_lo], 1), preferred_element_type=F32)
    low = jnp.dot(x_lo, c_hi, preferred_element_type=F32)
    return 2.0 * (wide[:, :n] + wide[:, n:] + low) - a


def head_kernel(core_ref, mine_ref, other_ref, base_out, x_out, d_out):
    d = cosines_of(core_ref[0], mine_ref, other_ref)
    d_out[...] = d
    base_out[...], x_out[...] = rough_inverse(d, jnp.transpose(d))


def tail_kernel(base_ref, x_ref, d_ref, *refs):
    *blocks, a_out = refs
    a, b = both_blocks(blocks)
    a_out[...] = first_block(a, b, *corrected(base_ref[...], x_ref[...], d_ref[...]))


def late_kernel(m_ref, md_ref, *refs):
    *blocks, a_out = refs
    a, b = both_blocks(blocks)
    a_out[...] = first_block(a, b, m_ref[...], md_ref[...])


def second_kernel(core_ref, mine_ref, other_ref, own_ref, *refs):
    *blocks, b_out, m_out, md_out, mine_out, other_out, cross_ref = refs
    d = cosines_of(1 - core_ref[0], mine_ref, other_ref)
    dt = jnp.transpose(d)
    a, b = both_blocks(blocks)
    turned = left3(a - times3(left3(b), right3(dt)))
    own = own_ref[...]
    m, md = corrected(*rough_inverse(d, dt), d)
    b = b + 2.0 * times3(turned, right3(md))
    message(
        squares(own), squares(b), cross_of(own, b), core_ref[0], cross_ref, mine_out, other_out
    )
    b_out[...] = b
    m_out[...] = m
    md_out[...] = md


def last_kernel(core_ref, mine_ref, other_ref, own_ref, *refs):
    *blocks, out_ref, b_ref, sems = refs
    rows, n = own_ref.shape
    copies = [pltpu.make_async_copy(own_ref, out_ref.at[:, :n], sems.at[CHUNKS])]
    copies[0].start()
    d = cosines_of(1 - core_ref[0], mine_ref, other_ref)
    dt = jnp.transpose(d)
    a, b = both_blocks(blocks)
    turned = left3(a - times3(left3(b), right3(dt)))
    _, md = corrected(*rough_inverse(d, dt), d)
    right = right3(md)
    size = rows // CHUNKS
    for i in range(CHUNKS):
        part = slice(i * size, (i + 1) * size)
        b_ref[part] = b[part] + 2.0 * times3(turned[part], right)
        copy = pltpu.make_async_copy(b_ref.at[part], out_ref.at[part, n:], sems.at[i])
        copy.start()
        copies.append(copy)
    for copy in copies:
        copy.wait()


def near(x):
    return pltpu.with_memory_space_constraint(x, pltpu.VMEM)


def vmem_call(kernel, shapes, arrays, core=None, scratch=(), **options):
    specs = [pl.BlockSpec(memory_space=pltpu.VMEM)] * len(arrays)
    arrays = [near(x) for x in arrays]
    if core is not None:
        specs = [pl.BlockSpec(memory_space=pltpu.SMEM)] + specs
        arrays = [core] + arrays
    return pl.pallas_call(
        kernel, out_shape=shapes, in_specs=specs, scratch_shapes=scratch, **options
    )(*arrays)


def message_shapes(n):
    half = pltpu.VMEM((n // 2 + PAD, n), F32)
    return [half, half], [pltpu.VMEM((n + 2 * PAD, n), F32)]


def load(core, panel, n):
    halves, scratch = message_shapes(n)
    return pl.pallas_call(
        load_kernel,
        out_shape=[pltpu.VMEM(panel.shape, F32), *halves],
        in_specs=[pl.BlockSpec(memory_space=pltpu.SMEM), pl.BlockSpec(memory_space=pl.ANY)],
        scratch_shapes=[*scratch, pltpu.SemaphoreType.DMA],
        name="load",
    )(core, panel)


def turn_head(core, halves, n):
    squares = [pltpu.VMEM((n, n), F32)] * 3
    return vmem_call(head_kernel, squares, halves, core)


def turn_tail(squares, blocks, n):
    block = pltpu.VMEM((blocks[0].shape[0], n), F32)
    return vmem_call(tail_kernel, block, [*squares, *blocks])


def turn_late(m, md, blocks, n):
    block = pltpu.VMEM((blocks[0].shape[0], n), F32)
    return vmem_call(late_kernel, block, [m, md, *blocks])


def turn_second(core, halves, own, blocks, n):
    message_out, scratch = message_shapes(n)
    square = pltpu.VMEM((n, n), F32)
    shapes = [pltpu.VMEM(own.shape, F32), square, square, *message_out]
    arrays = [*halves, own, *blocks]
    return vmem_call(second_kernel, shapes, arrays, core, scratch)


def turn_last(core, halves, own, blocks):
    rows, n = own.shape
    return vmem_call(
        last_kernel,
        jax.ShapeDtypeStruct((rows, 2 * n), F32),
        [*halves, own, *blocks],
        core,
        [pltpu.VMEM((rows, n), F32), pltpu.SemaphoreType.DMA((CHUNKS + 1,))],
        out_specs=pl.BlockSpec(memory_space=pl.ANY),
    )


def from_row(x, source):
    devices = range(lax.axis_size("row"))
    line = len(devices) // QUAD
    route = []
    for i in devices:
        z, y_lo, core = source(i // QUAD, i // 2 % 2, i % 2)
        route.append((z % line * QUAD + y_lo * 2 + core, i))
    return lax.ppermute(x, "row", route)


def mate(z, y, c):
    return z, y, 1 - c


def owner(chip):
    def source(z, y, c):
        other_z, other_y = chip(z, y)
        return other_z, other_y, (c + z + y + other_z + other_y) % 2

    return source


def side(z):
    return 1 if z % 2 else -1


def summed_halves(mine, other, y_last):
    incoming = from_row(other, mate)
    x = mine + incoming
    next_z = from_row(x, owner(lambda z, y: (z ^ 1, y)))
    if y_last:
        x = x + next_z
    else:
        next_y = from_row(x, owner(lambda z, y: (z, 1 - y)))
        next_zy = from_row(x, owner(lambda z, y: (z ^ 1, 1 - y)))
        x = ((x + next_z) + next_y) + next_zy
    by_one = from_row(x, owner(lambda z, y: (z + side(z), y)))
    by_two = from_row(x, owner(lambda z, y: (z - 2 * side(z), y)))
    by_three = from_row(x, owner(lambda z, y: (z + 3 * side(z), y)))
    x = ((x + by_one) + by_two) + by_three
    if y_last:
        x = x + from_row(x, owner(lambda z, y: (z, 1 - y)))
    return x


def with_other(half):
    return [half, from_row(half, mate)]


def shifted(block):
    devices = range(lax.axis_size("pair"))
    route = [((i - 1) % len(devices), i) for i in devices]
    return lax.ppermute(block, "pair", route)


def hopped_over(half):
    pairs = lax.axis_size("pair")
    route = []
    for row in range(lax.axis_size("row")):
        for pair in range(pairs):
            source = (row ^ 1) * pairs + (pair - 1) % pairs
            route.append((source, row * pairs + pair))
    return lax.ppermute(half, ("row", "pair"), route)


def local(panel):
    n = panel.shape[1] // 2
    row = lax.axis_index("row")
    core = ((row ^ (row >> 1) ^ (row >> 2)) & 1).astype(jnp.int32).reshape(1)
    for step in range(STEPS):
        if step == 0:
            own, mine, other = load(core, panel, n)
            before = [shifted(own)]
            own = [own]
        else:
            second = shifted(b)
            before = [turn_late(m, md, before, n), second]
        half = summed_halves(mine, other, y_last=step == 0)
        hopped = hopped_over(half)
        own_halves = with_other(half)
        squares = turn_head(core, own_halves, n)
        halves = with_other(hopped)
        a = turn_tail(squares, own, n)
        if step + 1 == STEPS:
            return turn_last(core, halves, a, before)
        b, m, md, mine, other = turn_second(core, halves, a, before, n)
        own = [a, b]


def solution(mesh):
    return jax.shard_map(
        local,
        mesh=mesh,
        in_specs=(P("row", "pair"),),
        out_specs=P("row", "pair"),
        check_vma=False,
    )
```

```python
import jax
import jax.numpy as jnp
from jax import lax
from jax.experimental import pallas as pl
from jax.experimental.pallas import tpu as pltpu
from jax.sharding import PartitionSpec as P


STEPS = 3

BF16 = jnp.bfloat16
F32 = jnp.float32
HIGH = lax.Precision.HIGHEST

QUAD = 4
PAD = 8
CHUNKS = 4


def split(x):
    hi = x.astype(BF16)
    return hi, (x - hi.astype(F32)).astype(BF16)


def left3(x):
    return jnp.concatenate(split(x), 1)


def right3(x):
    hi, lo = split(x)
    top = jnp.concatenate([hi, lo], 1)
    low = jnp.concatenate([hi, jnp.zeros_like(hi)], 1)
    return jnp.concatenate([top, low], 0)


def times3(left, right):
    out = jnp.dot(left, right, preferred_element_type=F32)
    n = out.shape[1] // 2
    return out[:, :n] + out[:, n:]


def times(a, b):
    return jnp.dot(a, b, precision=HIGH, preferred_element_type=F32)


def quarter_cosines(cross, diag_a, diag_b):
    shape = cross.shape
    scale_a = lax.rsqrt(diag_a + 1e-06)
    scale_b = lax.rsqrt(diag_b + 1e-06)
    return 0.25 * (cross * jnp.transpose(jnp.broadcast_to(scale_a, shape)) * scale_b)


def identity(n):
    row = lax.broadcasted_iota(jnp.int32, (n, n), 0)
    column = lax.broadcasted_iota(jnp.int32, (n, n), 1)
    return jnp.where(row == column, 1.0, 0.0).astype(F32)


def rough_inverse(d, dt):
    n = d.shape[0]
    eye = identity(n)
    base = eye + times(d, dt)
    top = 1.0 + 1.001 * (0.25 * n) ** 2
    start = 2.0 / (1.0 + top)
    gap = (top - 1.0) / (top + 1.0)
    y = start * base
    x = None
    while gap > 0.05:
        z = 2.0 * eye - y
        stretch = 2.0 / (2.0 - gap * gap)
        right = right3(z)
        if x is None:
            y = stretch * times3(left3(y), right)
            x = (stretch * start) * z
        else:
            both = stretch * times3(jnp.concatenate([left3(x), left3(y)], 0), right)
            x, y = both[:n], both[n:]
        gap = gap * gap / (2.0 - gap * gap)
    left = eye - times3(left3(x), right3(base))
    x = x + times3(left3(left), right3(x))
    return base, x


def corrected(base, x, d):
    n = d.shape[0]
    wide = times(x, jnp.concatenate([base, d], 1))
    left = identity(n) - wide[:, :n]
    both = jnp.concatenate([x, wide[:, n:]], 1)
    both = both + times3(left3(left), right3(both))
    return both[:, :n], both[:, n:]


def message(diag_a, diag_b, cross, core, cross_ref, mine_ref, other_ref):
    n = cross.shape[0]
    half = n // 2
    step = half + PAD
    cross_ref[:half] = cross[:half]
    cross_ref[step : step + half] = cross[half:]
    cross_ref[half:step] = jnp.broadcast_to(diag_a, (PAD, n))
    cross_ref[step + half :] = jnp.broadcast_to(diag_b, (PAD, n))
    mine_ref[...] = cross_ref[pl.ds(pl.multiple_of(core * step, 8), step), :]
    other_ref[...] = cross_ref[pl.ds(pl.multiple_of((1 - core) * step, 8), step), :]


def both_blocks(refs):
    if len(refs) == 1:
        n = refs[0].shape[1] // 2
        return refs[0][:, :n], refs[0][:, n:]
    return refs[0][...], refs[1][...]


def cross_of(a, b):
    n = a.shape[1]
    a_hi, a_lo = split(jnp.transpose(a))
    b_hi, b_lo = split(b)
    wide = jnp.dot(a_hi, jnp.concatenate([b_hi, b_lo], 1), preferred_element_type=F32)
    return wide[:, :n] + wide[:, n:] + jnp.dot(a_lo, b_hi, preferred_element_type=F32)


def squares(block):
    return jnp.sum(block * block, 0, keepdims=True)


def load_kernel(core_ref, panel_ref, near_ref, mine_ref, other_ref, cross_ref, sem):
    copy = pltpu.make_async_copy(panel_ref, near_ref, sem)
    copy.start()
    copy.wait()
    a, b = both_blocks([near_ref])
    message(squares(a), squares(b), cross_of(a, b), core_ref[0], cross_ref, mine_ref, other_ref)


def cosines_of(owned, mine_ref, other_ref):
    half = mine_ref.shape[0] - PAD
    first = owned == 0
    mine = mine_ref[...]
    other = other_ref[...]
    low = jnp.where(first, mine, other)
    high = jnp.where(first, other, mine)
    cross = jnp.concatenate([low[:half], high[:half]], 0)
    return quarter_cosines(cross, low[half : half + 1], high[half : half + 1])


def first_block(a, b, m, md):
    n = m.shape[0]
    x_hi, x_lo = split(jnp.concatenate([a, b], 1))
    c_hi, c_lo = split(jnp.concatenate([m, -jnp.transpose(md)], 0))
    wide = jnp.dot(x_hi, jnp.concatenate([c_hi, c_lo], 1), preferred_element_type=F32)
    low = jnp.dot(x_lo, c_hi, preferred_element_type=F32)
    return 2.0 * (wide[:, :n] + wide[:, n:] + low) - a


def head_kernel(core_ref, mine_ref, other_ref, base_out, x_out, d_out):
    d = cosines_of(core_ref[0], mine_ref, other_ref)
    d_out[...] = d
    base_out[...], x_out[...] = rough_inverse(d, jnp.transpose(d))


def tail_kernel(base_ref, x_ref, d_ref, *refs):
    *blocks, a_out = refs
    a, b = both_blocks(blocks)
    a_out[...] = first_block(a, b, *corrected(base_ref[...], x_ref[...], d_ref[...]))


def late_kernel(m_ref, md_ref, *refs):
    *blocks, a_out = refs
    a, b = both_blocks(blocks)
    a_out[...] = first_block(a, b, m_ref[...], md_ref[...])


def second_kernel(core_ref, mine_ref, other_ref, own_ref, *refs):
    *blocks, b_out, m_out, md_out, mine_out, other_out, cross_ref = refs
    d = cosines_of(core_ref[0], mine_ref, other_ref)
    dt = jnp.transpose(d)
    a, b = both_blocks(blocks)
    turned = left3(a - times3(left3(b), right3(dt)))
    own = own_ref[...]
    m, md = corrected(*rough_inverse(d, dt), d)
    b = b + 2.0 * times3(turned, right3(md))
    message(
        squares(own), squares(b), cross_of(own, b), core_ref[0], cross_ref, mine_out, other_out
    )
    b_out[...] = b
    m_out[...] = m
    md_out[...] = md


def last_kernel(core_ref, mine_ref, other_ref, own_ref, *refs):
    *blocks, out_ref, b_ref, sems = refs
    rows, n = own_ref.shape
    copies = [pltpu.make_async_copy(own_ref, out_ref.at[:, :n], sems.at[CHUNKS])]
    copies[0].start()
    d = cosines_of(core_ref[0], mine_ref, other_ref)
    dt = jnp.transpose(d)
    a, b = both_blocks(blocks)
    turned = left3(a - times3(left3(b), right3(dt)))
    _, md = corrected(*rough_inverse(d, dt), d)
    right = right3(md)
    size = rows // CHUNKS
    for i in range(CHUNKS):
        part = slice(i * size, (i + 1) * size)
        b_ref[part] = b[part] + 2.0 * times3(turned[part], right)
        copy = pltpu.make_async_copy(b_ref.at[part], out_ref.at[part, n:], sems.at[i])
        copy.start()
        copies.append(copy)
    for copy in copies:
        copy.wait()


def near(x):
    return pltpu.with_memory_space_constraint(x, pltpu.VMEM)


def vmem_call(kernel, shapes, arrays, core=None, scratch=(), **options):
    specs = [pl.BlockSpec(memory_space=pltpu.VMEM)] * len(arrays)
    arrays = [near(x) for x in arrays]
    if core is not None:
        specs = [pl.BlockSpec(memory_space=pltpu.SMEM)] + specs
        arrays = [core] + arrays
    return pl.pallas_call(
        kernel, out_shape=shapes, in_specs=specs, scratch_shapes=scratch, **options
    )(*arrays)


def message_shapes(n):
    half = pltpu.VMEM((n // 2 + PAD, n), F32)
    return [half, half], [pltpu.VMEM((n + 2 * PAD, n), F32)]


def load(core, panel, n):
    halves, scratch = message_shapes(n)
    return pl.pallas_call(
        load_kernel,
        out_shape=[pltpu.VMEM(panel.shape, F32), *halves],
        in_specs=[pl.BlockSpec(memory_space=pltpu.SMEM), pl.BlockSpec(memory_space=pl.ANY)],
        scratch_shapes=[*scratch, pltpu.SemaphoreType.DMA],
        name="load",
    )(core, panel)


def turn_head(core, halves, n):
    squares = [pltpu.VMEM((n, n), F32)] * 3
    return vmem_call(head_kernel, squares, halves, core)


def turn_tail(squares, blocks, n):
    block = pltpu.VMEM((blocks[0].shape[0], n), F32)
    return vmem_call(tail_kernel, block, [*squares, *blocks])


def turn_late(m, md, blocks, n):
    block = pltpu.VMEM((blocks[0].shape[0], n), F32)
    return vmem_call(late_kernel, block, [m, md, *blocks])


def turn_second(core, halves, own, blocks, n):
    message_out, scratch = message_shapes(n)
    square = pltpu.VMEM((n, n), F32)
    shapes = [pltpu.VMEM(own.shape, F32), square, square, *message_out]
    arrays = [*halves, own, *blocks]
    return vmem_call(second_kernel, shapes, arrays, core, scratch)


def turn_last(core, halves, own, blocks):
    rows, n = own.shape
    return vmem_call(
        last_kernel,
        jax.ShapeDtypeStruct((rows, 2 * n), F32),
        [*halves, own, *blocks],
        core,
        [pltpu.VMEM((rows, n), F32), pltpu.SemaphoreType.DMA((CHUNKS + 1,))],
        out_specs=pl.BlockSpec(memory_space=pl.ANY),
    )


def from_row(x, source):
    devices = range(lax.axis_size("row"))
    line = len(devices) // QUAD
    route = []
    for i in devices:
        z, y_lo, core = source(i // QUAD, i // 2 % 2, i % 2)
        route.append((z % line * QUAD + y_lo * 2 + core, i))
    return lax.ppermute(x, "row", route)


def mate(z, y, c):
    return z, y, 1 - c


def owner(chip):
    def source(z, y, c):
        other_z, other_y = chip(z, y)
        return other_z, other_y, (c + z + y + other_z + other_y) % 2

    return source


def side(z):
    return 1 if z % 2 else -1


def summed_halves(mine, other, y_last):
    incoming = from_row(other, mate)
    x = mine + incoming
    next_z = from_row(x, owner(lambda z, y: (z ^ 1, y)))
    if y_last:
        x = x + next_z
    else:
        next_y = from_row(x, owner(lambda z, y: (z, 1 - y)))
        next_zy = from_row(x, owner(lambda z, y: (z ^ 1, 1 - y)))
        x = ((x + next_z) + next_y) + next_zy
    by_one = from_row(x, owner(lambda z, y: (z + side(z), y)))
    by_two = from_row(x, owner(lambda z, y: (z - 2 * side(z), y)))
    by_three = from_row(x, owner(lambda z, y: (z + 3 * side(z), y)))
    x = ((x + by_one) + by_two) + by_three
    if y_last:
        x = x + from_row(x, owner(lambda z, y: (z, 1 - y)))
    return x


def with_other(half):
    return [half, from_row(half, mate)]


def shifted(block):
    devices = range(lax.axis_size("pair"))
    route = [((i - 1) % len(devices), i) for i in devices]
    return lax.ppermute(block, "pair", route)


def hopped_over(half):
    pairs = lax.axis_size("pair")
    route = []
    for row in range(lax.axis_size("row")):
        for pair in range(pairs):
            source = (row ^ 3) * pairs + (pair - 1) % pairs
            route.append((source, row * pairs + pair))
    return lax.ppermute(half, ("row", "pair"), route)


def local(panel):
    n = panel.shape[1] // 2
    row = lax.axis_index("row")
    core = ((row ^ (row >> 1) ^ (row >> 2)) & 1).astype(jnp.int32).reshape(1)
    for step in range(STEPS):
        if step == 0:
            own, mine, other = load(core, panel, n)
            before = [shifted(own)]
            own = [own]
        else:
            second = shifted(b)
            before = [turn_late(m, md, before, n), second]
        half = summed_halves(mine, other, y_last=step == 0)
        hopped = hopped_over(half)
        own_halves = with_other(half)
        squares = turn_head(core, own_halves, n)
        halves = with_other(hopped)
        a = turn_tail(squares, own, n)
        if step + 1 == STEPS:
            return turn_last(core, halves, a, before)
        b, m, md, mine, other = turn_second(core, halves, a, before, n)
        own = [a, b]


def solution(mesh):
    return jax.shard_map(
        local,
        mesh=mesh,
        in_specs=(P("row", "pair"),),
        out_specs=P("row", "pair"),
        check_vma=False,
    )
```

```python
import jax
import jax.numpy as jnp
from jax import lax
from jax.experimental import pallas as pl
from jax.experimental.pallas import tpu as pltpu
from jax.sharding import PartitionSpec as P


STEPS = 3

BF16 = jnp.bfloat16
F32 = jnp.float32
HIGH = lax.Precision.HIGHEST

QUAD = 4
PAD = 8
CHUNKS = 4


def split(x):
    hi = x.astype(BF16)
    return hi, (x - hi.astype(F32)).astype(BF16)


def left3(x):
    return jnp.concatenate(split(x), 1)


def right3(x):
    hi, lo = split(x)
    top = jnp.concatenate([hi, lo], 1)
    low = jnp.concatenate([hi, jnp.zeros_like(hi)], 1)
    return jnp.concatenate([top, low], 0)


def times3(left, right):
    out = jnp.dot(left, right, preferred_element_type=F32)
    n = out.shape[1] // 2
    return out[:, :n] + out[:, n:]


def times(a, b):
    return jnp.dot(a, b, precision=HIGH, preferred_element_type=F32)


def quarter_cosines(cross, diag_a, diag_b):
    shape = cross.shape
    scale_a = lax.rsqrt(diag_a + 1e-06)
    scale_b = lax.rsqrt(diag_b + 1e-06)
    return 0.25 * (cross * jnp.transpose(jnp.broadcast_to(scale_a, shape)) * scale_b)


def identity(n):
    row = lax.broadcasted_iota(jnp.int32, (n, n), 0)
    column = lax.broadcasted_iota(jnp.int32, (n, n), 1)
    return jnp.where(row == column, 1.0, 0.0).astype(F32)


def rough_inverse(d, dt):
    n = d.shape[0]
    eye = identity(n)
    base = eye + times(d, dt)
    top = 1.0 + 1.001 * (0.25 * n) ** 2
    start = 2.0 / (1.0 + top)
    gap = (top - 1.0) / (top + 1.0)
    y = start * base
    x = None
    while gap > 0.05:
        z = 2.0 * eye - y
        stretch = 2.0 / (2.0 - gap * gap)
        right = right3(z)
        if x is None:
            y = stretch * times3(left3(y), right)
            x = (stretch * start) * z
        else:
            both = stretch * times3(jnp.concatenate([left3(x), left3(y)], 0), right)
            x, y = both[:n], both[n:]
        gap = gap * gap / (2.0 - gap * gap)
    left = eye - times3(left3(x), right3(base))
    x = x + times3(left3(left), right3(x))
    return base, x


def corrected(base, x, d):
    n = d.shape[0]
    wide = times(x, jnp.concatenate([base, d], 1))
    left = identity(n) - wide[:, :n]
    both = jnp.concatenate([x, wide[:, n:]], 1)
    both = both + times3(left3(left), right3(both))
    return both[:, :n], both[:, n:]


def message(diag_a, diag_b, cross, core, cross_ref, mine_ref, other_ref):
    n = cross.shape[0]
    half = n // 2
    step = half + PAD
    cross_ref[:half] = cross[:half]
    cross_ref[step : step + half] = cross[half:]
    cross_ref[half:step] = jnp.broadcast_to(diag_a, (PAD, n))
    cross_ref[step + half :] = jnp.broadcast_to(diag_b, (PAD, n))
    mine_ref[...] = cross_ref[pl.ds(pl.multiple_of(core * step, 8), step), :]
    other_ref[...] = cross_ref[pl.ds(pl.multiple_of((1 - core) * step, 8), step), :]


def both_blocks(refs):
    if len(refs) == 1:
        n = refs[0].shape[1] // 2
        return refs[0][:, :n], refs[0][:, n:]
    return refs[0][...], refs[1][...]


def cross_of(a, b):
    n = a.shape[1]
    a_hi, a_lo = split(jnp.transpose(a))
    b_hi, b_lo = split(b)
    wide = jnp.dot(a_hi, jnp.concatenate([b_hi, b_lo], 1), preferred_element_type=F32)
    return wide[:, :n] + wide[:, n:] + jnp.dot(a_lo, b_hi, preferred_element_type=F32)


def squares(block):
    return jnp.sum(block * block, 0, keepdims=True)


def load_kernel(core_ref, panel_ref, near_ref, mine_ref, other_ref, cross_ref, sem):
    copy = pltpu.make_async_copy(panel_ref, near_ref, sem)
    copy.start()
    copy.wait()
    a, b = both_blocks([near_ref])
    message(squares(a), squares(b), cross_of(a, b), core_ref[0], cross_ref, mine_ref, other_ref)


def cosines_of(owned, mine_ref, other_ref):
    half = mine_ref.shape[0] - PAD
    first = owned == 0
    mine = mine_ref[...]
    other = other_ref[...]
    low = jnp.where(first, mine, other)
    high = jnp.where(first, other, mine)
    cross = jnp.concatenate([low[:half], high[:half]], 0)
    return quarter_cosines(cross, low[half : half + 1], high[half : half + 1])


def first_block(a, b, m, md):
    n = m.shape[0]
    x_hi, x_lo = split(jnp.concatenate([a, b], 1))
    c_hi, c_lo = split(jnp.concatenate([m, -jnp.transpose(md)], 0))
    wide = jnp.dot(x_hi, jnp.concatenate([c_hi, c_lo], 1), preferred_element_type=F32)
    low = jnp.dot(x_lo, c_hi, preferred_element_type=F32)
    return 2.0 * (wide[:, :n] + wide[:, n:] + low) - a


def head_kernel(core_ref, mine_ref, other_ref, base_out, x_out, d_out):
    d = cosines_of(core_ref[0], mine_ref, other_ref)
    d_out[...] = d
    base_out[...], x_out[...] = rough_inverse(d, jnp.transpose(d))


def tail_kernel(base_ref, x_ref, d_ref, *refs):
    *blocks, a_out = refs
    a, b = both_blocks(blocks)
    a_out[...] = first_block(a, b, *corrected(base_ref[...], x_ref[...], d_ref[...]))


def late_kernel(m_ref, md_ref, *refs):
    *blocks, a_out = refs
    a, b = both_blocks(blocks)
    a_out[...] = first_block(a, b, m_ref[...], md_ref[...])


def second_kernel(core_ref, mine_ref, other_ref, own_ref, *refs):
    *blocks, b_out, m_out, md_out, mine_out, other_out, cross_ref = refs
    d = cosines_of(core_ref[0], mine_ref, other_ref)
    dt = jnp.transpose(d)
    a, b = both_blocks(blocks)
    turned = left3(a - times3(left3(b), right3(dt)))
    own = own_ref[...]
    m, md = corrected(*rough_inverse(d, dt), d)
    b = b + 2.0 * times3(turned, right3(md))
    message(
        squares(own), squares(b), cross_of(own, b), core_ref[0], cross_ref, mine_out, other_out
    )
    b_out[...] = b
    m_out[...] = m
    md_out[...] = md


def last_kernel(core_ref, mine_ref, other_ref, own_ref, *refs):
    *blocks, out_ref, b_ref, sems = refs
    rows, n = own_ref.shape
    copies = [pltpu.make_async_copy(own_ref, out_ref.at[:, :n], sems.at[CHUNKS])]
    copies[0].start()
    d = cosines_of(core_ref[0], mine_ref, other_ref)
    dt = jnp.transpose(d)
    a, b = both_blocks(blocks)
    turned = left3(a - times3(left3(b), right3(dt)))
    _, md = corrected(*rough_inverse(d, dt), d)
    right = right3(md)
    size = rows // CHUNKS
    for i in range(CHUNKS):
        part = slice(i * size, (i + 1) * size)
        b_ref[part] = b[part] + 2.0 * times3(turned[part], right)
        copy = pltpu.make_async_copy(b_ref.at[part], out_ref.at[part, n:], sems.at[i])
        copy.start()
        copies.append(copy)
    for copy in copies:
        copy.wait()


def near(x):
    return pltpu.with_memory_space_constraint(x, pltpu.VMEM)


def vmem_call(kernel, shapes, arrays, core=None, scratch=(), **options):
    specs = [pl.BlockSpec(memory_space=pltpu.VMEM)] * len(arrays)
    arrays = [near(x) for x in arrays]
    if core is not None:
        specs = [pl.BlockSpec(memory_space=pltpu.SMEM)] + specs
        arrays = [core] + arrays
    return pl.pallas_call(
        kernel, out_shape=shapes, in_specs=specs, scratch_shapes=scratch, **options
    )(*arrays)


def message_shapes(n):
    half = pltpu.VMEM((n // 2 + PAD, n), F32)
    return [half, half], [pltpu.VMEM((n + 2 * PAD, n), F32)]


def load(core, panel, n):
    halves, scratch = message_shapes(n)
    return pl.pallas_call(
        load_kernel,
        out_shape=[pltpu.VMEM(panel.shape, F32), *halves],
        in_specs=[pl.BlockSpec(memory_space=pltpu.SMEM), pl.BlockSpec(memory_space=pl.ANY)],
        scratch_shapes=[*scratch, pltpu.SemaphoreType.DMA],
        name="load",
    )(core, panel)


def turn_head(core, halves, n):
    squares = [pltpu.VMEM((n, n), F32)] * 3
    return vmem_call(head_kernel, squares, halves, core)


def turn_tail(squares, blocks, n):
    block = pltpu.VMEM((blocks[0].shape[0], n), F32)
    return vmem_call(tail_kernel, block, [*squares, *blocks])


def turn_late(m, md, blocks, n):
    block = pltpu.VMEM((blocks[0].shape[0], n), F32)
    return vmem_call(late_kernel, block, [m, md, *blocks])


def turn_second(core, halves, own, blocks, n):
    message_out, scratch = message_shapes(n)
    square = pltpu.VMEM((n, n), F32)
    shapes = [pltpu.VMEM(own.shape, F32), square, square, *message_out]
    arrays = [*halves, own, *blocks]
    return vmem_call(second_kernel, shapes, arrays, core, scratch)


def turn_last(core, halves, own, blocks):
    rows, n = own.shape
    return vmem_call(
        last_kernel,
        jax.ShapeDtypeStruct((rows, 2 * n), F32),
        [*halves, own, *blocks],
        core,
        [pltpu.VMEM((rows, n), F32), pltpu.SemaphoreType.DMA((CHUNKS + 1,))],
        out_specs=pl.BlockSpec(memory_space=pl.ANY),
    )


def from_row(x, source):
    devices = range(lax.axis_size("row"))
    line = len(devices) // QUAD
    route = []
    for i in devices:
        z, y_lo, core = source(i // QUAD, i // 2 % 2, i % 2)
        route.append((z % line * QUAD + y_lo * 2 + core, i))
    return lax.ppermute(x, "row", route)


def mate(z, y, c):
    return z, y, 1 - c


def owner(chip):
    def source(z, y, c):
        half = (c + z + y) % 2
        side = 1 if (z + half) % 2 else -1
        other_z, other_y = chip(z, y, side)
        return other_z, other_y, (half + other_z + other_y) % 2

    return source


def summed_halves(mine, other, y_last):
    incoming = from_row(other, mate)
    x = mine + incoming
    next_z = from_row(x, owner(lambda z, y, side: (z - side, y)))
    if y_last:
        x = x + next_z
    else:
        next_y = from_row(x, owner(lambda z, y, side: (z, 1 - y)))
        next_zy = from_row(x, owner(lambda z, y, side: (z - side, 1 - y)))
        x = ((x + next_z) + next_y) + next_zy
    by_one = from_row(x, owner(lambda z, y, side: (z + side, y)))
    by_two = from_row(x, owner(lambda z, y, side: (z - 2 * side, y)))
    by_three = from_row(x, owner(lambda z, y, side: (z + 3 * side, y)))
    x = ((x + by_one) + by_two) + by_three
    if y_last:
        x = x + from_row(x, owner(lambda z, y, side: (z, 1 - y)))
    return x


def with_other(half):
    return [half, from_row(half, mate)]


def shifted(block):
    devices = range(lax.axis_size("pair"))
    route = [((i - 1) % len(devices), i) for i in devices]
    return lax.ppermute(block, "pair", route)


def hopped_over(half):
    pairs = lax.axis_size("pair")
    route = []
    for row in range(lax.axis_size("row")):
        for pair in range(pairs):
            source = (row ^ 3) * pairs + (pair - 1) % pairs
            route.append((source, row * pairs + pair))
    return lax.ppermute(half, ("row", "pair"), route)


def local(panel):
    n = panel.shape[1] // 2
    row = lax.axis_index("row")
    core = ((row ^ (row >> 1) ^ (row >> 2)) & 1).astype(jnp.int32).reshape(1)
    for step in range(STEPS):
        if step == 0:
            own, mine, other = load(core, panel, n)
            before = [shifted(own)]
            own = [own]
        else:
            second = shifted(b)
            before = [turn_late(m, md, before, n), second]
        half = summed_halves(mine, other, y_last=step == 0)
        hopped = hopped_over(half)
        own_halves = with_other(half)
        squares = turn_head(core, own_halves, n)
        halves = with_other(hopped)
        a = turn_tail(squares, own, n)
        if step + 1 == STEPS:
            return turn_last(core, halves, a, before)
        b, m, md, mine, other = turn_second(core, halves, a, before, n)
        own = [a, b]


def solution(mesh):
    return jax.shard_map(
        local,
        mesh=mesh,
        in_specs=(P("row", "pair"),),
        out_specs=P("row", "pair"),
        check_vma=False,
    )
```

```python
import jax
import jax.numpy as jnp
from jax import lax
from jax.experimental import pallas as pl
from jax.experimental.pallas import tpu as pltpu
from jax.sharding import PartitionSpec as P


STEPS = 3

BF16 = jnp.bfloat16
F32 = jnp.float32
HIGH = lax.Precision.HIGHEST

QUAD = 4
PAD = 8
CHUNKS = 2


def split(x):
    hi = x.astype(BF16)
    return hi, (x - hi.astype(F32)).astype(BF16)


def left3(x):
    return jnp.concatenate(split(x), 1)


def right3(x):
    hi, lo = split(x)
    top = jnp.concatenate([hi, lo], 1)
    low = jnp.concatenate([hi, jnp.zeros_like(hi)], 1)
    return jnp.concatenate([top, low], 0)


def times3(left, right):
    out = jnp.dot(left, right, preferred_element_type=F32)
    n = out.shape[1] // 2
    return out[:, :n] + out[:, n:]


def times(a, b):
    return jnp.dot(a, b, precision=HIGH, preferred_element_type=F32)


def quarter_cosines(cross, diag_a, diag_b):
    shape = cross.shape
    scale_a = lax.rsqrt(diag_a + 1e-06)
    scale_b = lax.rsqrt(diag_b + 1e-06)
    return 0.25 * (cross * jnp.transpose(jnp.broadcast_to(scale_a, shape)) * scale_b)


def identity(n):
    row = lax.broadcasted_iota(jnp.int32, (n, n), 0)
    column = lax.broadcasted_iota(jnp.int32, (n, n), 1)
    return jnp.where(row == column, 1.0, 0.0).astype(F32)


def rough_inverse(d, dt):
    n = d.shape[0]
    eye = identity(n)
    base = eye + times3(left3(d), right3(dt))
    top = 1.0 + 1.001 * (0.25 * n) ** 2
    start = 2.0 / (1.0 + top)
    gap = (top - 1.0) / (top + 1.0)
    y = start * base
    x = None
    while gap > 0.05:
        z = 2.0 * eye - y
        stretch = 2.0 / (2.0 - gap * gap)
        right = right3(z)
        gap = gap * gap / (2.0 - gap * gap)
        if x is None:
            y = stretch * times3(left3(y), right)
            x = (stretch * start) * z
        elif gap > 0.05:
            both = stretch * times3(jnp.concatenate([left3(x), left3(y)], 0), right)
            x, y = both[:n], both[n:]
        else:
            x = stretch * times3(left3(x), right)
    left = eye - times3(left3(x), right3(base))
    x = x + times3(left3(left), right3(x))
    return base, x


def corrected(base, x, d):
    n = d.shape[0]
    wide = times(x, jnp.concatenate([base, d], 1))
    left = identity(n) - wide[:, :n]
    both = jnp.concatenate([x, wide[:, n:]], 1)
    both = both + times3(left3(left), right3(both))
    return both[:, :n], both[:, n:]


def message(diag_a, diag_b, cross, core, cross_ref, mine_ref, other_ref):
    n = cross.shape[0]
    half = n // 2
    step = half + PAD
    cross_ref[:half] = cross[:half]
    cross_ref[step : step + half] = cross[half:]
    cross_ref[half:step] = jnp.broadcast_to(diag_a, (PAD, n))
    cross_ref[step + half :] = jnp.broadcast_to(diag_b, (PAD, n))
    mine_ref[...] = cross_ref[pl.ds(pl.multiple_of(core * step, 8), step), :]
    other_ref[...] = cross_ref[pl.ds(pl.multiple_of((1 - core) * step, 8), step), :]


def both_blocks(refs):
    if len(refs) == 1:
        n = refs[0].shape[1] // 2
        return refs[0][:, :n], refs[0][:, n:]
    return refs[0][...], refs[1][...]


def cross_of(a, b):
    n = a.shape[1]
    a_hi, a_lo = split(jnp.transpose(a))
    b_hi, b_lo = split(b)
    wide = jnp.dot(a_hi, jnp.concatenate([b_hi, b_lo], 1), preferred_element_type=F32)
    return wide[:, :n] + wide[:, n:] + jnp.dot(a_lo, b_hi, preferred_element_type=F32)


def squares(block):
    return jnp.sum(block * block, 0, keepdims=True)


def load_kernel(core_ref, panel_ref, near_ref, mine_ref, other_ref, cross_ref, sem):
    copy = pltpu.make_async_copy(panel_ref, near_ref, sem)
    copy.start()
    copy.wait()
    a, b = both_blocks([near_ref])
    message(squares(a), squares(b), cross_of(a, b), core_ref[0], cross_ref, mine_ref, other_ref)


def cosines_of(owned, mine_ref, other_ref):
    half = mine_ref.shape[0] - PAD
    first = owned == 0
    mine = mine_ref[...]
    other = other_ref[...]
    low = jnp.where(first, mine, other)
    high = jnp.where(first, other, mine)
    cross = jnp.concatenate([low[:half], high[:half]], 0)
    return quarter_cosines(cross, low[half : half + 1], high[half : half + 1])


def first_block(a, b, m, md):
    n = m.shape[0]
    x_hi, x_lo = split(jnp.concatenate([a, b], 1))
    c_hi, c_lo = split(jnp.concatenate([m, -jnp.transpose(md)], 0))
    wide = jnp.dot(x_hi, jnp.concatenate([c_hi, c_lo], 1), preferred_element_type=F32)
    low = jnp.dot(x_lo, c_hi, preferred_element_type=F32)
    return 2.0 * (wide[:, :n] + wide[:, n:] + low) - a


def head_kernel(core_ref, mine_ref, other_ref, base_out, x_out, d_out):
    d = cosines_of(core_ref[0], mine_ref, other_ref)
    d_out[...] = d
    base_out[...], x_out[...] = rough_inverse(d, jnp.transpose(d))


def tail_kernel(base_ref, x_ref, d_ref, *refs):
    *blocks, a_out = refs
    a, b = both_blocks(blocks)
    a_out[...] = first_block(a, b, *corrected(base_ref[...], x_ref[...], d_ref[...]))


def late_kernel(m_ref, md_ref, *refs):
    *blocks, a_out = refs
    a, b = both_blocks(blocks)
    a_out[...] = first_block(a, b, m_ref[...], md_ref[...])


def second_kernel(core_ref, mine_ref, other_ref, own_ref, *refs):
    *blocks, b_out, m_out, md_out, mine_out, other_out, cross_ref = refs
    d = cosines_of(core_ref[0], mine_ref, other_ref)
    dt = jnp.transpose(d)
    a, b = both_blocks(blocks)
    turned = left3(a - times3(left3(b), right3(dt)))
    own = own_ref[...]
    m, md = corrected(*rough_inverse(d, dt), d)
    b = b + 2.0 * times3(turned, right3(md))
    message(
        squares(own), squares(b), cross_of(own, b), core_ref[0], cross_ref, mine_out, other_out
    )
    b_out[...] = b
    m_out[...] = m
    md_out[...] = md


def last_kernel(core_ref, mine_ref, other_ref, own_ref, *refs):
    *blocks, out_ref, b_ref, sems = refs
    rows, n = own_ref.shape
    copies = [pltpu.make_async_copy(own_ref, out_ref.at[:, :n], sems.at[CHUNKS])]
    copies[0].start()
    d = cosines_of(core_ref[0], mine_ref, other_ref)
    dt = jnp.transpose(d)
    a, b = both_blocks(blocks)
    turned = left3(a - times3(left3(b), right3(dt)))
    _, md = corrected(*rough_inverse(d, dt), d)
    right = right3(md)
    size = rows // CHUNKS
    for i in range(CHUNKS):
        part = slice(i * size, (i + 1) * size)
        b_ref[part] = b[part] + 2.0 * times3(turned[part], right)
        copy = pltpu.make_async_copy(b_ref.at[part], out_ref.at[part, n:], sems.at[i])
        copy.start()
        copies.append(copy)
    for copy in copies:
        copy.wait()


def near(x):
    return pltpu.with_memory_space_constraint(x, pltpu.VMEM)


def vmem_call(kernel, shapes, arrays, core=None, scratch=(), **options):
    specs = [pl.BlockSpec(memory_space=pltpu.VMEM)] * len(arrays)
    arrays = [near(x) for x in arrays]
    if core is not None:
        specs = [pl.BlockSpec(memory_space=pltpu.SMEM)] + specs
        arrays = [core] + arrays
    return pl.pallas_call(
        kernel, out_shape=shapes, in_specs=specs, scratch_shapes=scratch, **options
    )(*arrays)


def message_shapes(n):
    half = pltpu.VMEM((n // 2 + PAD, n), F32)
    return [half, half], [pltpu.VMEM((n + 2 * PAD, n), F32)]


def load(core, panel, n):
    halves, scratch = message_shapes(n)
    return pl.pallas_call(
        load_kernel,
        out_shape=[pltpu.VMEM(panel.shape, F32), *halves],
        in_specs=[pl.BlockSpec(memory_space=pltpu.SMEM), pl.BlockSpec(memory_space=pl.ANY)],
        scratch_shapes=[*scratch, pltpu.SemaphoreType.DMA],
        name="load",
    )(core, panel)


def turn_head(core, halves, n):
    squares = [pltpu.VMEM((n, n), F32)] * 3
    return vmem_call(head_kernel, squares, halves, core)


def turn_tail(squares, blocks, n):
    block = pltpu.VMEM((blocks[0].shape[0], n), F32)
    return vmem_call(tail_kernel, block, [*squares, *blocks])


def turn_late(m, md, blocks, n):
    block = pltpu.VMEM((blocks[0].shape[0], n), F32)
    return vmem_call(late_kernel, block, [m, md, *blocks])


def turn_second(core, halves, own, blocks, n):
    message_out, scratch = message_shapes(n)
    square = pltpu.VMEM((n, n), F32)
    shapes = [pltpu.VMEM(own.shape, F32), square, square, *message_out]
    arrays = [*halves, own, *blocks]
    return vmem_call(second_kernel, shapes, arrays, core, scratch)


def turn_last(core, halves, own, blocks):
    rows, n = own.shape
    return vmem_call(
        last_kernel,
        jax.ShapeDtypeStruct((rows, 2 * n), F32),
        [*halves, own, *blocks],
        core,
        [pltpu.VMEM((rows, n), F32), pltpu.SemaphoreType.DMA((CHUNKS + 1,))],
        out_specs=pl.BlockSpec(memory_space=pl.ANY),
    )


def from_row(x, source):
    devices = range(lax.axis_size("row"))
    line = len(devices) // QUAD
    route = []
    for i in devices:
        z, y_lo, core = source(i // QUAD, i // 2 % 2, i % 2)
        route.append((z % line * QUAD + y_lo * 2 + core, i))
    return lax.ppermute(x, "row", route)


def mate(z, y, c):
    return z, y, 1 - c


def owner(chip):
    def source(z, y, c):
        other_z, other_y = chip(z, y)
        return other_z, other_y, (c + z + y + other_z + other_y) % 2

    return source


def side(z):
    return 1 if z % 2 else -1


def summed_halves(mine, other, y_last):
    incoming = from_row(other, mate)
    x = mine + incoming
    next_z = from_row(x, owner(lambda z, y: (z ^ 1, y)))
    if y_last:
        x = x + next_z
    else:
        next_y = from_row(x, owner(lambda z, y: (z, 1 - y)))
        next_zy = from_row(x, owner(lambda z, y: (z ^ 1, 1 - y)))
        x = ((x + next_z) + next_y) + next_zy
    by_one = from_row(x, owner(lambda z, y: (z + side(z), y)))
    by_two = from_row(x, owner(lambda z, y: (z - 2 * side(z), y)))
    by_three = from_row(x, owner(lambda z, y: (z + 3 * side(z), y)))
    x = ((x + by_one) + by_two) + by_three
    if y_last:
        x = x + from_row(x, owner(lambda z, y: (z, 1 - y)))
    return x


def with_other(half):
    return [half, from_row(half, mate)]


def shifted(block):
    devices = range(lax.axis_size("pair"))
    route = [((i - 1) % len(devices), i) for i in devices]
    return lax.ppermute(block, "pair", route)


def hopped_over(half):
    pairs = lax.axis_size("pair")
    route = []
    for row in range(lax.axis_size("row")):
        for pair in range(pairs):
            source = (row ^ 3) * pairs + (pair - 1) % pairs
            route.append((source, row * pairs + pair))
    return lax.ppermute(half, ("row", "pair"), route)


def local(panel):
    n = panel.shape[1] // 2
    row = lax.axis_index("row")
    core = ((row ^ (row >> 1) ^ (row >> 2)) & 1).astype(jnp.int32).reshape(1)
    for step in range(STEPS):
        if step == 0:
            own, mine, other = load(core, panel, n)
            before = [shifted(own)]
            own = [own]
        else:
            second = shifted(b)
            before = [turn_late(m, md, before, n), second]
        half = summed_halves(mine, other, y_last=step == 0)
        hopped = hopped_over(half)
        own_halves = with_other(half)
        squares = turn_head(core, own_halves, n)
        halves = with_other(hopped)
        a = turn_tail(squares, own, n)
        if step + 1 == STEPS:
            return turn_last(core, halves, a, before)
        b, m, md, mine, other = turn_second(core, halves, a, before, n)
        own = [a, b]


def solution(mesh):
    return jax.shard_map(
        local,
        mesh=mesh,
        in_specs=(P("row", "pair"),),
        out_specs=P("row", "pair"),
        check_vma=False,
    )
```
